32 devices in a mesh: lat: 16 (over z, y, core), rad: 2 (over x).
Axes of the slice: x: 2, y: 2, z: 4, core: 2. Of those that a mesh axis runs over, the one named last changes fastest.
Arguments:
- displacement: float32 [256, 8, 2048], P('lat', 'rad'), may hold values from -3 to 3
- memory: float32 [256, 8, 2048], P('lat', 'rad'), may hold values from -3 to 3
- ice_class: int32 [256, 2048], P('lat'), may hold values from 0 to 7
- material: int32 [256, 8], P('lat', 'rad'), may hold values from 0 to 7
- mu_table: float32 [8], replicated, may hold values from 0.5 to 4
- decay_table: float32 [8], replicated, may hold values from 0.2 to 0.95
- contrast_table: float32 [8], replicated, may hold values from 0.5 to 2
- gravity_kernel: float32 [256, 8, 8], P('lat', 'rad'), may hold values from -2 to 2
Outputs:
- displacement_out: float32 [256, 8, 2048], P('lat', 'rad')
- memory_out: float32 [256, 8, 2048], P('lat', 'rad')
- potential: float32 [256, 8, 2048], P('lat', 'rad')
The draws below stay inside these ranges and needn't reach their ends.
All inputs are finite; a program needn't handle non-finite values.
Results may differ from the reference program's by a relative error of at most 0.0028.
Values sent between devices are 32-bit elements; how exact they have to be, the bound alone decides.
A program may use at most 64 MiB of HBM per device.

```python
import math
import jax
import jax.numpy as jnp
from jax import lax

NLON = 2048
MODES = 256
NDEG = 256
NMAT = 8
NCLASS = 8
NLAT = 256
NR = 8


def place_ends(entries, rng, least, top_value):
    spot = [jax.random.randint(jax.random.fold_in(rng, axis), (), 0, length) for axis, length in enumerate(entries.shape)]
    main_axis = entries.shape.index(max(entries.shape))
    neighbour = spot[:main_axis] + [(spot[main_axis] + 1) % entries.shape[main_axis]] + spot[main_axis + 1:]
    return entries.at[tuple(spot)].set(least).at[tuple(neighbour)].set(top_value)


def block_scale(rng, extent, cuts, low, high):
    factor_of, own = 1.0, jax.random.fold_in(rng, 6)
    for position, blocks in cuts:
        draws = jnp.exp(jax.random.uniform(jax.random.fold_in(own, position), (blocks,), jnp.float32, low / len(cuts), high / len(cuts)))
        factor_of = factor_of * jnp.repeat(draws, extent[position] // blocks).reshape([-1 if axis == position else 1 for axis in range(len(extent))])
    return factor_of


def centred(rng, shape, deviation, limit, pieces=(), held_as=jnp.bfloat16):
    values = jax.random.normal(rng, shape, jnp.float32) * deviation
    if len(pieces) > 0:
        values = block_scale(rng, shape, pieces, -0.22, 0.18) * values
    return jnp.clip(values, min=-limit, max=limit).astype(held_as)


def setup_inputs(seed: int = 0) -> dict:
    keys = jax.random.split(jax.random.key(seed), 9)
    return {
        "displacement": centred(keys[0], (NLAT, NR, NLON), 0.5, 3.0, ((0, 16), (1, 2)), jnp.float32),
        "memory": centred(keys[1], (NLAT, NR, NLON), 0.5, 3.0, ((0, 16), (1, 2)), jnp.float32),
        "ice_class": place_ends(jax.random.randint(keys[2], (NLAT, NLON), 0, NCLASS), jax.random.fold_in(keys[2], 1), 0, NCLASS - 1).astype(jnp.int32),
        "material": place_ends(jax.random.randint(keys[3], (NLAT, NR), 0, NMAT), jax.random.fold_in(keys[3], 1), 0, NMAT - 1).astype(jnp.int32),
        "mu_table": jnp.clip(jnp.exp(jax.random.uniform(keys[4], (NMAT,), jnp.float32, math.log(0.5), math.log(4.0))), 0.5, 4.0),
        "decay_table": jnp.clip(jax.random.uniform(keys[5], (NMAT,), jnp.float32, 0.2, 0.95), 0.2, 0.95),
        "contrast_table": jnp.clip(jax.random.uniform(keys[6], (NMAT,), jnp.float32, 0.5, 2.0), 0.5, 2.0),
        "gravity_kernel": centred(keys[7], (NDEG, NR, NR), NR ** -0.5, 2.0, ((0, 16), (1, 2)), jnp.float32),
    }


load_scale = 0.5
kappa_shift = 0.5
relax_factor = 0.8
coupling = 2.0

def lookup(material, table):
    onehot = (material[:, :, None] == jnp.arange(table.shape[0], dtype=jnp.int32)[None, None, :]).astype(jnp.float32)
    return lax.optimization_barrier(jnp.sum(onehot * table[None, None, :], axis=-1))

def fourier_table(nlon, modes):
    longitude = jnp.arange(nlon, dtype=jnp.int32)
    order = jnp.arange(modes, dtype=jnp.int32)
    phase = (longitude[:, None] * order[None, :] % nlon).astype(jnp.float32)
    angle = phase * (2.0 * jnp.pi / nlon)
    scale = jnp.sqrt(jnp.float32(2.0) / nlon)
    return scale * jnp.concatenate([jnp.cos(angle), jnp.sin(angle)], axis=1)

def legendre(cosine, count):

    def step(carry, degree):
        before, current = carry
        nextone = ((2.0 * degree + 1.0) * cosine * current - degree * before) / (degree + 1.0)
        return ((current, nextone), current * jnp.sqrt(degree + 0.5))
    start = (jnp.zeros_like(cosine), jnp.ones_like(cosine))
    _, rows = lax.scan(step, start, jnp.arange(count, dtype=jnp.float32))
    return rows

def sweep(field, memory, source, stiff, decay):
    padded = jnp.pad(field, ((1, 1), (1, 1), (0, 0)))
    beside = padded[2:, 1:-1] + padded[:-2, 1:-1] + padded[1:-1, 2:] + padded[1:-1, :-2]
    beside = beside + jnp.roll(field, 1, axis=2) + jnp.roll(field, -1, axis=2)
    diagonal = stiff * (6.0 + kappa_shift)
    applied = diagonal * field - stiff * beside
    update = relax_factor * (source - memory - applied) / diagonal
    return (field + update, decay * memory + stiff * update)

def reference(displacement, memory, ice_class, material, mu_table, decay_table, contrast_table, gravity_kernel):
    stiff = lookup(material, mu_table)[:, :, None]
    decay = lookup(material, decay_table)[:, :, None]
    contrast = lookup(material, contrast_table)[:, :, None]
    layer_pos = (jnp.arange(NR, dtype=jnp.float32) + 1.0) / NR
    source = load_scale * ice_class.astype(jnp.float32)[:, None, :] * layer_pos[None, :, None]
    field, mem = (displacement, memory)
    for step in range(3):
        field, mem = sweep(field, mem, source, stiff, decay)
    rho = contrast * field
    rho = rho - jnp.sum(rho) / (NLAT * NR * NLON)
    table = fourier_table(NLON, MODES)
    cols = 2 * MODES
    spectra = jnp.dot(rho.reshape(NLAT * NR, NLON), table, precision=lax.Precision.HIGHEST).reshape(NLAT, NR * cols)
    theta = (jnp.arange(NLAT, dtype=jnp.float32) + 0.5) * (jnp.pi / NLAT)
    basis = legendre(jnp.cos(theta), NDEG)
    weighted = basis * (jnp.pi / NLAT * jnp.sin(theta))[None, :]
    coef = jnp.dot(weighted, spectra, precision=lax.Precision.HIGHEST).reshape(NDEG, NR, cols)
    phi = jnp.einsum('nab,nbk->nak', gravity_kernel, coef, precision=lax.Precision.HIGHEST)
    synth = jnp.dot(basis.T, phi.reshape(NDEG, NR * cols), precision=lax.Precision.HIGHEST)
    potential = jnp.dot(synth.reshape(NLAT * NR, cols), table.T, precision=lax.Precision.HIGHEST).reshape(NLAT, NR, NLON)
    loaded = source + coupling * potential
    for step in range(3):
        field, mem = sweep(field, mem, loaded, stiff, decay)
    return (field, mem, potential)
```

```python
import jax
import jax.numpy as jnp
import numpy as np
from jax import lax
from jax.experimental import pallas as pl
from jax.experimental.pallas import tpu as pltpu
from jax.sharding import PartitionSpec as P

MODES = 256


load_scale = 0.5
kappa_shift = 0.5
relax_factor = 0.8
coupling = 2.0
HIGH = lax.Precision.HIGH


def lookup(material, table):
    onehot = (
        material[:, :, None] == jnp.arange(table.shape[0], dtype=jnp.int32)[None, None, :]
    ).astype(jnp.float32)
    return jnp.sum(onehot * table[None, None, :], axis=-1)


def fourier_parts(nlon, modes, minor=128):
    order = np.arange(modes)
    parts = []
    for place in (np.arange(nlon // minor) * minor, np.arange(minor)):
        angle = (place[:, None] * order[None, :] % nlon) * (2.0 * np.pi / nlon)
        parts += [np.cos(angle), np.sin(angle)]
    scale = np.sqrt(2.0 / nlon)
    return [(part * f).astype(np.float32) for part, f in zip(parts, (scale, scale, 1.0, 1.0))]


def fourier_table(nlon, modes):
    ca, sa, cb, sb = lax.optimization_barrier([jnp.asarray(p) for p in fourier_parts(nlon, modes)])
    ca, sa, cb, sb = ca[:, None], sa[:, None], cb[None], sb[None]
    cos = (ca * cb - sa * sb).reshape(nlon, modes)
    sin = (sa * cb + ca * sb).reshape(nlon, modes)
    return jnp.concatenate([cos, sin], axis=1)


def legendre(lat, degrees):
    theta = np.pi * (np.arange(lat) + 0.5) / lat
    cosine = np.cos(theta)
    before, current, rows = np.zeros(lat), np.ones(lat), []
    for n in range(degrees):
        rows.append(current * np.sqrt(n + 0.5))
        before, current = current, ((2.0 * n + 1.0) * cosine * current - n * before) / (n + 1.0)
    basis = np.stack(rows)
    weighted = basis * (np.pi / lat * np.sin(theta))[None, :]
    return basis, weighted


def sweeps_kernel(steps, gather, *refs):
    if gather:
        f_ref, m_ref, s_ref, stiff_ref, decay_ref, g_ref, f_out, m_out, g_out, *refs = refs
        f_buf, face, lat_in, rad_in, send, recv, g_in, g_send, g_recv = refs
    else:
        f_ref, m_ref, s_ref, stiff_ref, decay_ref, f_out, m_out, *refs = refs
        f_buf, face, lat_in, rad_in, send, recv = refs
    layers, rows, nlon = f_ref.shape
    lat_n, rad_n = lax.axis_size("lat"), lax.axis_size("rad")
    lat, rad = lax.axis_index("lat"), lax.axis_index("rad")
    north = (lax.rem(lat + lat_n - 1, lat_n), rad)
    south = (lax.rem(lat + 1, lat_n), rad)
    below = (lat, lax.rem(rad + rad_n - 1, rad_n))
    above = (lat, lax.rem(rad + 1, rad_n))
    if gather:
        peers = [(lax.rem(lat + d, lat_n), rad) for d in range(1, lat_n)] + [below, above]
    else:
        peers = [north, south, below, above]
    barrier = pltpu.get_barrier_semaphore()
    for peer in peers:
        pl.semaphore_signal(barrier, inc=1, device_id=peer, device_id_type=pl.DeviceIdType.MESH)
    pl.semaphore_wait(barrier, len(peers))

    def remote(src, dst, send_sem, recv_sem, peer):
        copy = pltpu.make_async_remote_copy(
            src_ref=src, dst_ref=dst, send_sem=send_sem, recv_sem=recv_sem,
            device_id=peer, device_id_type=pl.DeviceIdType.MESH,
        )
        copy.start()
        return copy

    weight = relax_factor / (6.0 + kappa_shift)
    w_north = jnp.where(lat > 0, weight, 0.0)
    w_south = jnp.where(lat < lat_n - 1, weight, 0.0)
    w_below = jnp.where(rad > 0, weight, 0.0)
    w_above = jnp.where(rad < rad_n - 1, weight, 0.0)
    row = lax.broadcasted_iota(jnp.int32, (rows, nlon), 0)
    gathered = []
    for step in range(steps):
        old = f_ref if step == 0 else f_buf.at[step - 1]
        new = f_out if step == steps - 1 else f_buf.at[step]
        old_m = m_ref if step == 0 else m_out
        for r in range(layers):
            face[step, 0, r : r + 1, :] = old[r, 0:1, :]
            face[step, 1, r : r + 1, :] = old[r, rows - 1 : rows, :]
        copies = [
            remote(old.at[0], rad_in.at[step, 1], send.at[step, 0], recv.at[step, 0], below),
            remote(old.at[layers - 1], rad_in.at[step, 0], send.at[step, 1], recv.at[step, 1], above),
            remote(face.at[step, 0], lat_in.at[step, 1], send.at[step, 2], recv.at[step, 2], north),
            remote(face.at[step, 1], lat_in.at[step, 0], send.at[step, 3], recv.at[step, 3], south),
        ]
        if gather and step == 0:
            gathered = [
                remote(g_ref, g_in.at[lat], g_send.at[d], g_recv.at[d], peers[d - 1])
                for d in range(1, lat_n)
            ]
        for r in range(layers):
            f, m = old[r], old_m[r]
            beside = pltpu.roll(f, 1, 1) + pltpu.roll(f, nlon - 1, 1)
            beside += jnp.where(row == 0, 0.0, pltpu.roll(f, 1, 0))
            beside += jnp.where(row == rows - 1, 0.0, pltpu.roll(f, rows - 1, 0))
            if r > 0:
                beside += old[r - 1]
            if r < layers - 1:
                beside += old[r + 1]
            stiff = stiff_ref[r]
            update = (s_ref[r] - m) * (weight / stiff) - relax_factor * f + weight * beside
            new[r] = f + update
            m_out[r] = decay_ref[r] * m + stiff * update
        for copy in copies:
            copy.wait()
        for r, slot, w in ((0, 0, w_below), (layers - 1, 1, w_above)):
            extra = w * rad_in[step, slot]
            new[r] += extra
            m_out[r] += stiff_ref[r] * extra
        for r in range(layers):
            for j, slot, w in ((0, 0, w_north), (rows - 1, 1, w_south)):
                extra = w * lat_in[step, slot, r : r + 1, :]
                new[r, j : j + 1, :] += extra
                m_out[r, j : j + 1, :] += stiff_ref[r, j : j + 1, :] * extra
    if gather:
        for copy in gathered:
            copy.wait()
        g_in[lat] = g_ref[...]
        g_out[...] = g_in[...]


def sweeps(steps, field, memory, source, stiff, decay, gravity=None):
    gather = gravity is not None
    layers, rows, nlon = field.shape
    block = jax.ShapeDtypeStruct(field.shape, jnp.float32)
    operands, out = [field, memory, source, stiff, decay], [block, block]
    dma, f32 = pltpu.SemaphoreType.DMA, jnp.float32
    scratch = [
        pltpu.VMEM((steps - 1, layers, rows, nlon), f32),
        pltpu.VMEM((steps, 2, layers, nlon), f32),
        pltpu.VMEM((steps, 2, layers, nlon), f32),
        pltpu.VMEM((steps, 2, rows, nlon), f32),
        dma((steps, 4)),
        dma((steps, 4)),
    ]
    if gather:
        lat_n = lax.axis_size("lat")
        every = (lat_n,) + gravity.shape
        operands.append(gravity)
        out.append(jax.ShapeDtypeStruct(every, f32))
        scratch += [pltpu.VMEM(every, f32), dma((lat_n,)), dma((lat_n,))]
    vmem = pl.BlockSpec(memory_space=pltpu.VMEM)

    def kernel(*refs):
        sweeps_kernel(steps, gather, *refs)

    return pl.pallas_call(
        kernel,
        out_shape=out,
        in_specs=[vmem] * len(operands),
        out_specs=[vmem] * len(out),
        scratch_shapes=scratch,
        compiler_params=pltpu.CompilerParams(
            collective_id=0 if gather else 1, has_side_effects=True
        ),
    )(*operands)


LANES = 128
CHUNKS = 4
SWEEPS = 3


def split_np(x):
    x = np.asarray(x, np.float32)
    hi = x.astype(jnp.bfloat16)
    return hi, (x - hi.astype(np.float32)).astype(jnp.bfloat16)


def split(x):
    hi = x.astype(jnp.bfloat16)
    return hi, (x - hi.astype(jnp.float32)).astype(jnp.bfloat16)


def dot3(left, right, transposed=False):
    dims = (((1,), (1 if transposed else 0,)), ((), ()))

    def one(a, b):
        return lax.dot_general(a, b, dims, preferred_element_type=jnp.float32)

    return one(left[0], right[0]) + (one(left[0], right[1]) + one(left[1], right[0]))


def radix_tables(nlon, modes):
    quarter, per = nlon // 4, modes // 4
    place = np.arange(quarter)[:, None]

    def waves(k):
        order = k + 4 * np.arange(per)[None, :]
        angle = (place * order % nlon) * (2.0 * np.pi / nlon)
        return np.sqrt(2.0 / nlon) * np.cos(angle), np.sqrt(2.0 / nlon) * np.sin(angle)

    (c0, s0), (c1, s1), (c2, s2), (c3, s3) = (waves(k) for k in range(4))
    even = np.concatenate([c0, s0, c2, s2], axis=1)
    odd = np.concatenate(
        [np.concatenate([c1, s1, c3, s3], axis=1), np.concatenate([-s1, c1, s3, -c3], axis=1)],
        axis=0,
    )
    return even, odd


def column_orders(modes):
    per = np.arange(modes // 4)
    return np.concatenate([k + 4 * per for k in (0, 0, 2, 2, 1, 1, 3, 3)])


def swap_groups(parts, width):
    parts, step = list(parts), 1
    lane = lax.broadcasted_iota(jnp.int32, parts[0].shape, 1)
    while step < len(parts):
        low = (lane // (width * step)) % 2 == 0
        for g in range(len(parts)):
            if (g // step) % 2 == 0:
                a, b = parts[g], parts[g + step]
                parts[g] = jnp.where(low, a, pltpu.roll(b, width * step, 1))
                parts[g + step] = jnp.where(low, pltpu.roll(a, LANES - width * step, 1), b)
        step *= 2
    return parts


def fused_kernel(
    u_ref, m_ref, ice_ref, stiff_ref, decay_ref, mat_ref, grav_ref,
    even_hi, even_lo, odd_hi, odd_lo, fwd_hi, fwd_lo, inv_hi, inv_lo,
    shift_ref, spread_ref, expand_ref, repeat_ref, mu_ref, dec_ref, con_ref,
    u_out, m_out, p_out,
    ubuf, sbuf, x_in, lat_out, lat_in, g_in, mat_in, pack_out, pack_in, ice_out, ice_in,
    back_out, back_in, gexp, par,
    x_send, x_recv, l_send, l_recv, g_send, g_recv, t_send, t_recv,
    a_send, a_recv, i_send, i_recv, b_send, b_recv,
):
    f32 = jnp.float32
    layers, rows, nlon = u_ref.shape
    lat_n, rad_n = lax.axis_size("lat"), lax.axis_size("rad")
    lat, rad = lax.axis_index("lat"), lax.axis_index("rad")
    count = lat_n * rad_n
    me = lat * rad_n + rad
    total_lat, total_rad = lat_n * rows, rad_n * layers
    halves = rows // 8
    width = LANES // (halves * layers)
    tiles = count * width // LANES
    per_tile = LANES // width
    chunk = nlon // CHUNKS
    last = 2 * SWEEPS
    weight = relax_factor / (6.0 + kappa_shift)

    def device(index):
        return (index // rad_n, lax.rem(index, rad_n))

    def peer(d):
        return lax.rem(me + d, count)

    barrier = pltpu.get_barrier_semaphore()

    def greet(d, carry):
        pl.semaphore_signal(
            barrier, inc=1, device_id=device(peer(d)), device_id_type=pl.DeviceIdType.MESH
        )
        return carry

    lax.fori_loop(1, count, greet, 0)

    def remote(src, dst, send_sem, recv_sem, target):
        return pltpu.make_async_remote_copy(
            src_ref=src, dst_ref=dst, send_sem=send_sem, recv_sem=recv_sem,
            device_id=target, device_id_type=pl.DeviceIdType.MESH,
        )

    def to_all(src_of, dst, send_sem, recv_sem):
        def start(d, carry):
            q = peer(d)
            remote(src_of(q), dst.at[me], send_sem.at[d], recv_sem.at[d], device(q)).start()
            return carry

        lax.fori_loop(1, count, start, 0)

    def each(src_of, dst, send_sem, recv_sem, how):
        def wait(d, carry):
            q = peer(d)
            copy = remote(src_of(q), dst.at[me], send_sem.at[d], recv_sem.at[d], device(q))
            copy.wait_recv() if how == "recv" else copy.wait_send()
            return carry

        lax.fori_loop(1, count, wait, 0)

    sides = (
        (0, rad > 0, 0, (lat, jnp.maximum(rad - 1, 0))),
        (1, rad < rad_n - 1, layers - 1, (lat, jnp.minimum(rad + 1, rad_n - 1))),
    )

    def x_copy(s, side, k, r, target):
        cols = pl.ds(k * chunk, chunk)
        return remote(
            ubuf.at[s, r, :, cols], x_in.at[s, 1 - side, :, cols],
            x_send.at[s, side, k], x_recv.at[s, 1 - side, k], target,
        )

    poles = (
        (0, lat > 0, 0, (jnp.maximum(lat - 1, 0), rad)),
        (1, lat < lat_n - 1, rows - 1, (jnp.minimum(lat + 1, lat_n - 1), rad)),
    )

    def lat_copy(s, side, r, target):
        return remote(
            lat_out.at[s, side, r], lat_in.at[s, 1 - side, r],
            l_send.at[s, side, r], l_recv.at[s, 1 - side, r], target,
        )

    def send_lat(s, r):
        for side, there, j, target in poles:
            @pl.when(there)
            def _():
                lat_out[s, side, r] = ubuf[s, r, j : j + 1, :]
                lat_copy(s, side, r, target).start()

    def sweep(s, more):
        row = lax.broadcasted_iota(jnp.int32, (rows, nlon), 0)

        def inner(r):
            for side, there, _, target in poles:
                @pl.when(there)
                def _():
                    lat_copy(s, 1 - side, r, target).wait_recv()

            f, m = ubuf[s, r], m_out[r]
            beside = pltpu.roll(f, 1, 1) + pltpu.roll(f, nlon - 1, 1)
            beside += jnp.where(row == 0, lat_in[s, 0, r], pltpu.roll(f, 1, 0))
            beside += jnp.where(row == rows - 1, lat_in[s, 1, r], pltpu.roll(f, rows - 1, 0))
            if r > 0:
                beside += ubuf[s, r - 1]
            if r < layers - 1:
                beside += ubuf[s, r + 1]
            stiff = stiff_ref[r]
            update = (sbuf[r] - m) * (weight / stiff) - relax_factor * f + weight * beside
            ubuf[s + 1, r] = f + update
            m_out[r] = decay_ref[r] * m + stiff * update

        rest = list(range(1, layers - 1))
        inner(layers - 1)
        inner(0)
        for k in range(CHUNKS):
            for side, there, r, target in sides:
                @pl.when(there)
                def _():
                    cols = slice(k * chunk, (k + 1) * chunk)
                    x_copy(s, 1 - side, k, r, target).wait_recv()
                    extra = weight * x_in[s, side, :, cols]
                    ubuf[s + 1, r, :, cols] += extra
                    m_out[r, :, cols] += stiff_ref[r] * extra
                    if more is True:
                        x_copy(s + 1, side, k, r, target).start()
                    else:
                        @pl.when(more)
                        def _():
                            x_copy(s + 1, side, k, r, target).start()
            if k < len(rest):
                inner(rest[k])

        def faces():
            for r in range(layers):
                send_lat(s + 1, r)

        if more is True:
            faces()
        else:
            pl.when(more)(faces)

    m_out[...] = m_ref[...]
    ubuf[0] = u_ref[...]
    ice = ice_ref[...].astype(f32)
    for r in range(layers):
        pos = (rad * layers + (r + 1)).astype(f32) / total_rad
        sbuf[r] = (load_scale * pos) * ice
    for side, there, _, _ in poles:
        @pl.when(jnp.logical_not(there))
        def _():
            for s in range(last):
                lat_in[s, side] = jnp.zeros(lat_in.shape[2:], f32)
    g_in[me] = grav_ref[...]
    mat_in[me] = mat_ref[...]

    pl.semaphore_wait(barrier, count - 1)
    for k in range(CHUNKS):
        for side, there, r, target in sides:
            @pl.when(there)
            def _():
                x_copy(0, side, k, r, target).start()
    for r in range(layers):
        send_lat(0, r)
    to_all(lambda q: grav_ref, g_in, g_send, g_recv)
    to_all(lambda q: mat_ref, mat_in, t_send, t_recv)

    quarter = nlon // 4
    block = layers * rows

    def piece(a):
        cols = slice(a * quarter, (a + 1) * quarter)
        return jnp.concatenate(
            [
                u_ref[:, :, cols].reshape(block, quarter),
                m_ref[:, :, cols].reshape(block, quarter),
                ice_ref[:, cols].astype(f32),
            ],
            axis=0,
        )

    x0, x1, x2, x3 = (piece(a) for a in range(4))
    half = even_hi.shape[1] // 2
    both, diff = x0 + x2, x1 + x3
    odd = split(jnp.concatenate([x0 - x2, x1 - x3], axis=1))
    spectra = jnp.concatenate(
        [
            dot3(split(both + diff), (even_hi[:, :half], even_lo[:, :half])),
            dot3(split(both - diff), (even_hi[:, half:], even_lo[:, half:])),
            dot3(odd, (odd_hi[...], odd_lo[...])),
        ],
        axis=1,
    )

    parts = []
    for h in range(halves):
        for r in range(layers):
            at = r * rows + 8 * h
            parts.append(
                jnp.concatenate(
                    [
                        spectra[o + at : o + at + 8, t * LANES : (t + 1) * LANES]
                        for t in range(tiles)
                        for o in (0, block)
                    ],
                    axis=0,
                )
            )
    for p, part in enumerate(swap_groups(parts, width)):
        for t in range(tiles):
            pack_out[per_tile * t + p] = part[16 * t : 16 * (t + 1)]
    to_all(lambda q: pack_out.at[q], pack_in, a_send, a_recv)
    pack_in[me] = pack_out[me]

    sub8 = lax.broadcasted_iota(jnp.int32, (8, LANES), 0)
    group8 = lax.broadcasted_iota(jnp.int32, (8, LANES), 1) // width
    for t in range(tiles):
        cols = slice(t * LANES, (t + 1) * LANES)
        x = spectra[2 * block : 2 * block + 8, cols]
        for h in range(1, halves):
            at = 2 * block + 8 * h
            x = jnp.where(rad == h, spectra[at : at + 8, cols], x)
        for step in (1, 2, 4):
            sb, gb = (sub8 // step) % 2, (group8 // step) % 2
            up = pltpu.roll(pltpu.roll(x, 8 - step, 0), width * step, 1)
            down = pltpu.roll(pltpu.roll(x, step, 0), LANES - width * step, 1)
            x = jnp.where(sb == gb, x, jnp.where(gb == 1, up, down))
        for p in range(per_tile):
            ice_out[per_tile * t + p] = x[p : p + 1]
    to_all(lambda q: ice_out.at[q], ice_in, i_send, i_recv)
    ice_in[me] = ice_out[me]

    each(lambda q: grav_ref, g_in, g_send, g_recv, "recv")
    each(lambda q: mat_ref, mat_in, t_send, t_recv, "recv")
    degrees = fwd_hi.shape[0]
    lane = lax.broadcasted_iota(jnp.int32, (degrees, LANES), 1)
    srow = lax.broadcasted_iota(jnp.int32, (degrees, LANES), 0)
    held = LANES // (layers * total_rad)
    cut = lane // (layers * total_rad) == lax.rem(srow, held)
    repeat = repeat_ref[...]
    wide = []
    for x in range(rad_n):
        lines = split(
            jnp.concatenate([g_in[rad_n * i + x] for i in range(lat_n)], axis=0)
        )
        full = jnp.dot(repeat, lines[0], preferred_element_type=f32) + jnp.dot(
            repeat, lines[1], preferred_element_type=f32
        )
        wide.append(jnp.where(cut, full, 0.0))
    wide = split(jnp.concatenate(wide, axis=1))
    for d in range(total_rad):
        cols = slice(d * LANES, (d + 1) * LANES)
        gexp[:, cols] = jnp.dot(
            wide[0], expand_ref[:, cols], preferred_element_type=f32
        ) + jnp.dot(wide[1], expand_ref[:, cols], preferred_element_type=f32)

    jrow = lax.broadcasted_iota(jnp.int32, (rows, LANES), 0)
    jlane = (lax.broadcasted_iota(jnp.int32, (rows, LANES), 1) // layers) % rows
    ids = []
    for i in range(lat_n):
        line = mat_in[rad_n * i]
        for x in range(1, rad_n):
            line = line + mat_in[rad_n * i + x]
        ids.append(jnp.where(jrow == jlane, jnp.broadcast_to(line, (rows, LANES)), 0.0))
    ids = jnp.dot(
        jnp.concatenate(ids, axis=0).astype(jnp.bfloat16), spread_ref[...],
        preferred_element_type=f32,
    )
    for n, table in enumerate((mu_ref, dec_ref, con_ref)):
        value = jnp.zeros((total_lat, LANES), f32)
        for k in range(table.shape[0]):
            value = jnp.where(ids == k, table[k], value)
        par[n] = value

    def two(s, carry):
        sweep(s, True)
        return carry

    lax.fori_loop(0, SWEEPS - 1, two, 0)

    each(lambda q: pack_out.at[q], pack_in, a_send, a_recv, "recv")
    each(lambda q: ice_out.at[q], ice_in, i_send, i_recv, "recv")
    near = lax.broadcasted_iota(jnp.int32, (16, LANES), 1) < LANES // 2
    us, qs, ss = [], [], []
    sub = lax.broadcasted_iota(jnp.int32, (8, LANES), 0)
    for i in range(lat_n):
        a, b = pack_in[rad_n * i], pack_in[rad_n * i + 1]
        top = jnp.where(near, a, pltpu.roll(b, LANES // 2, 1))
        low = jnp.where(near, pltpu.roll(a, LANES // 2, 1), b)
        us += [top[:8], low[:8]]
        qs += [top[8:], low[8:]]
        for x in range(rad_n):
            ss.append(
                jnp.where(sub == group8, jnp.broadcast_to(ice_in[rad_n * i + x], (8, LANES)), 0.0)
            )
    u, q, s_hat = (jnp.concatenate(v, axis=0) for v in (us, qs, ss))
    step = width
    while step < LANES:
        s_hat = s_hat + pltpu.roll(s_hat, step, 1)
        step *= 2
    glane = lax.broadcasted_iota(jnp.int32, (total_lat, LANES), 1)
    grow = lax.broadcasted_iota(jnp.int32, (total_lat, LANES), 0)
    s_hat = s_hat * ((glane // width + 1).astype(f32) * (load_scale / total_rad))
    shift = shift_ref[pl.ds(me, 1), :]
    stiff, decay, contrast = par[0], par[1], par[2]
    scaled = weight / stiff
    for n in range(SWEEPS):
        beside = shift * u
        beside += jnp.where(grow == 0, 0.0, pltpu.roll(u, 1, 0))
        beside += jnp.where(grow == total_lat - 1, 0.0, pltpu.roll(u, total_lat - 1, 0))
        beside += jnp.where(glane < width, 0.0, pltpu.roll(u, width, 1))
        beside += jnp.where(glane >= LANES - width, 0.0, pltpu.roll(u, LANES - width, 1))
        update = (s_hat - q) * scaled - relax_factor * u + weight * beside
        u = u + update
        q = decay * q + stiff * update
    rho = contrast * u
    zero = jnp.logical_and(me == 0, lax.rem(glane, width) == 0)
    mean = jnp.sum(jnp.where(zero, rho, 0.0)) / (total_lat * total_rad)
    rho = rho - jnp.where(zero, mean, 0.0)
    coef = dot3((fwd_hi[...], fwd_lo[...]), split(rho))
    phi = gexp[:, :LANES] * coef
    for d in range(1, total_rad):
        phi += gexp[:, d * LANES : (d + 1) * LANES] * pltpu.roll(coef, width * d, 1)
    synth = dot3((inv_hi[...], inv_lo[...]), split(phi))
    near8 = lax.broadcasted_iota(jnp.int32, (8, LANES), 1) < LANES // 2
    for i in range(lat_n):
        a, b = synth[rows * i : rows * i + 8], synth[rows * i + 8 : rows * i + 16]
        back_out[rad_n * i] = jnp.where(near8, a, pltpu.roll(b, LANES // 2, 1))
        back_out[rad_n * i + 1] = jnp.where(near8, pltpu.roll(a, LANES // 2, 1), b)
    to_all(lambda q: back_out.at[q], back_in, b_send, b_recv)
    back_in[me] = back_out[me]

    sweep(SWEEPS - 1, True)

    each(lambda q: back_out.at[q], back_in, b_send, b_recv, "recv")
    parts = swap_groups(
        [
            jnp.concatenate([back_in[per_tile * t + p] for t in range(tiles)], axis=0)
            for p in range(per_tile)
        ],
        width,
    )
    lines = []
    for r in range(layers):
        for h in range(halves):
            part = parts[h * layers + r]
            lines.append(
                jnp.concatenate([part[8 * t : 8 * (t + 1)] for t in range(tiles)], axis=1)
            )
    z = jnp.concatenate(lines, axis=0)
    y0 = dot3(split(z[:, :half]), (even_hi[:, :half], even_lo[:, :half]), True)
    y2 = dot3(split(z[:, half : 2 * half]), (even_hi[:, half:], even_lo[:, half:]), True)
    y13 = dot3(split(z[:, 2 * half :]), (odd_hi[...], odd_lo[...]), True)
    alpha, beta = y13[:, :quarter], y13[:, quarter:]
    plus, minus = y0 + y2, y0 - y2
    for a, value in enumerate((plus + alpha, minus + beta, plus - alpha, minus - beta)):
        cols = slice(a * quarter, (a + 1) * quarter)
        value = value.reshape(layers, rows, quarter)
        p_out[:, :, cols] = value
        sbuf[:, :, cols] += coupling * value

    def rest(s, carry):
        sweep(s, s + 1 < last)
        return carry

    lax.fori_loop(SWEEPS, last, rest, 0)
    u_out[...] = ubuf[last]

    each(lambda q: grav_ref, g_in, g_send, g_recv, "send")
    each(lambda q: mat_ref, mat_in, t_send, t_recv, "send")
    each(lambda q: pack_out.at[q], pack_in, a_send, a_recv, "send")
    each(lambda q: ice_out.at[q], ice_in, i_send, i_recv, "send")
    each(lambda q: back_out.at[q], back_in, b_send, b_recv, "send")

    def drain(s, carry):
        for side, there, r, target in sides:
            @pl.when(there)
            def _():
                for k in range(CHUNKS):
                    x_copy(s, side, k, r, target).wait_send()
        for side, there, _, target in poles:
            @pl.when(there)
            def _():
                for r in range(layers):
                    lat_copy(s, side, r, target).wait_send()
        return carry

    lax.fori_loop(0, last, drain, 0)


def fused(displacement, memory, ice_class, stiff, decay, material, tables, gravity):
    lat_dev, r_dev, nlon = displacement.shape
    lat_n, rad_n = lax.axis_size("lat"), lax.axis_size("rad")
    count, total_lat, total_rad = lat_n * rad_n, lat_n * lat_dev, rad_n * r_dev
    degrees = gravity.shape[0] * lat_n
    width = 2 * MODES // count
    bf16, f32 = jnp.bfloat16, jnp.float32
    even, odd = (split_np(t) for t in radix_tables(nlon, MODES))
    basis, weighted = legendre(total_lat, degrees)
    fwd, inv = split_np(weighted), split_np(basis.T)
    orders = column_orders(MODES).reshape(count, width)
    shift = np.tile(2.0 * np.cos(2.0 * np.pi * orders / nlon), (1, total_rad)).astype(np.float32)
    spread = np.zeros((LANES, LANES))
    for x in range(rad_n):
        for j in range(lat_dev):
            for r in range(r_dev):
                at = (x * r_dev + r) * width
                spread[x * lat_dev * r_dev + j * r_dev + r, at : at + width] = 1.0
    held = LANES // (r_dev * total_rad)
    expand = np.zeros((rad_n, held, r_dev, total_rad, total_rad, total_rad, width))
    for x in range(rad_n):
        for r in range(r_dev):
            for d in range(total_rad):
                to = x * r_dev + r
                expand[x, :, r, (to - d) % total_rad, d, to, :] = 1.0
    expand = expand.reshape(rad_n * LANES, total_rad * LANES)
    repeat = np.repeat(np.eye(degrees // held), held, axis=0)
    rad = lax.axis_index("rad")
    ids = material.astype(f32).reshape(1, lat_dev * r_dev)
    ids = jnp.concatenate([jnp.where(rad == x, ids, 0.0) for x in range(rad_n)], axis=1)
    gravity = gravity.reshape(-1, LANES)
    lines = gravity.shape[0]
    operands = [
        displacement.transpose(1, 0, 2), memory.transpose(1, 0, 2), ice_class, stiff, decay, ids, gravity,
        *even, *odd, *fwd, *inv, shift,
        spread.astype(bf16), expand.astype(bf16), repeat.astype(bf16), *tables,
    ]
    operands = [jnp.asarray(x) for x in operands]
    vmem = pl.BlockSpec(memory_space=pltpu.VMEM)
    smem = pl.BlockSpec(memory_space=pltpu.SMEM)
    dma = pltpu.SemaphoreType.DMA
    steps = 2 * SWEEPS
    block = jax.ShapeDtypeStruct((r_dev, lat_dev, nlon), f32)
    out = pl.pallas_call(
        fused_kernel,
        out_shape=[block] * 3,
        in_specs=[vmem] * (len(operands) - len(tables)) + [smem] * len(tables),
        out_specs=[vmem] * 3,
        scratch_shapes=[
            pltpu.VMEM((steps + 1, r_dev, lat_dev, nlon), f32),
            pltpu.VMEM((r_dev, lat_dev, nlon), f32),
            pltpu.VMEM((steps, 2, lat_dev, nlon), f32),
            pltpu.VMEM((steps, 2, r_dev, 1, nlon), f32),
            pltpu.VMEM((steps, 2, r_dev, 1, nlon), f32),
            pltpu.VMEM((count, lines, LANES), f32),
            pltpu.VMEM((count, 1, LANES), f32),
            pltpu.VMEM((count, 16, LANES), f32),
            pltpu.VMEM((count, 16, LANES), f32),
            pltpu.VMEM((count, 1, LANES), f32),
            pltpu.VMEM((count, 1, LANES), f32),
            pltpu.VMEM((count, 8, LANES), f32),
            pltpu.VMEM((count, 8, LANES), f32),
            pltpu.VMEM((degrees, total_rad * LANES), f32),
            pltpu.VMEM((3, total_lat, LANES), f32),
            dma((steps, 2, CHUNKS)), dma((steps, 2, CHUNKS)),
            dma((steps, 2, r_dev)), dma((steps, 2, r_dev)),
        ] + [dma((count,))] * 10,
        compiler_params=pltpu.CompilerParams(collective_id=2, has_side_effects=True),
    )(*operands)
    return tuple(x.transpose(1, 0, 2) for x in out)


def fits(lat_dev, r_dev, total_rad, rad_n, count):
    width = 2 * MODES // count
    return (
        rad_n == 2
        and lat_dev == 16
        and width * count == 2 * MODES
        and width * total_rad == LANES
        and rad_n * lat_dev * r_dev == LANES
        and LANES % (r_dev * total_rad) == 0
    )


def per_device(
    displacement, memory, ice_class, material, mu_table, decay_table, contrast_table, gravity_kernel
):
    lat_dev, r_dev, nlon = displacement.shape
    lat_count = lax.axis_size("lat")
    rad_count = lax.axis_size("rad")
    rad_index = lax.axis_index("rad")
    total_lat = lat_count * lat_dev
    total_rad = rad_count * r_dev
    degrees = gravity_kernel.shape[0] * lat_count
    cols = 2 * MODES
    columns = cols // lat_count
    stiff = lookup(material.T, mu_table)[:, :, None]
    decay = lookup(material.T, decay_table)[:, :, None]
    contrast = lookup(material.T, contrast_table)[:, :, None]
    layer_pos = (rad_index * r_dev + jnp.arange(r_dev, dtype=jnp.int32) + 1).astype(
        jnp.float32
    ) / total_rad
    source = load_scale * ice_class.astype(jnp.float32)[None, :, :] * layer_pos[:, None, None]
    if fits(lat_dev, r_dev, total_rad, rad_count, lat_count * rad_count):
        tables = (mu_table, decay_table, contrast_table)
        return fused(
            displacement, memory, ice_class, stiff, decay, material, tables, gravity_kernel
        )
    basis, weighted = legendre(total_lat, degrees)
    projection = jnp.asarray(
        np.concatenate([weighted, np.ones((8, total_lat))]).astype(np.float32)
    )
    weight_sum = jnp.asarray(weighted.sum(axis=1).astype(np.float32))
    basis = jnp.asarray(basis.T.astype(np.float32))
    table = fourier_table(nlon, MODES)
    field, mem, kernel_every = sweeps(
        3,
        displacement.transpose(1, 0, 2),
        memory.transpose(1, 0, 2),
        source,
        stiff,
        decay,
        gravity_kernel.reshape(gravity_kernel.shape[0], -1),
    )
    kernel_every = kernel_every.reshape((degrees,) + gravity_kernel.shape[1:])
    rho = contrast * field
    spectra = jnp.dot(rho.reshape(lat_dev * r_dev, nlon), table, precision=HIGH)
    spread = lax.all_to_all(
        spectra.reshape(r_dev, lat_dev, cols).transpose(1, 0, 2), "lat", split_axis=2, concat_axis=0, tiled=True
    )
    coef_cols = jnp.dot(
        projection, spread.reshape(total_lat, r_dev * columns), precision=HIGH
    ).reshape(degrees + 8, r_dev, columns)
    coef_all = lax.all_gather(coef_cols, "rad", axis=1, tiled=True)
    first_order = (lax.axis_index("lat") * columns + jnp.arange(columns, dtype=jnp.int32)) == 0
    mean_row = jnp.sum(coef_all[degrees], axis=0) / (total_lat * total_rad)
    mean_row = jnp.where(first_order, mean_row, 0.0)
    coef_all = coef_all[:degrees] - weight_sum[:, None, None] * mean_row[None, None, :]
    phi_cols = jnp.sum(kernel_every[:, :, :, None] * coef_all[:, None, :, :], axis=2)
    synth_cols = jnp.dot(
        basis, phi_cols.reshape(degrees, r_dev * columns), precision=HIGH
    ).reshape(total_lat, r_dev, columns)
    synth = lax.all_to_all(synth_cols, "lat", split_axis=0, concat_axis=2, tiled=True)
    potential = lax.dot_general(
        synth.transpose(1, 0, 2).reshape(r_dev * lat_dev, cols), table, (((1,), (1,)), ((), ())), precision=HIGH
    ).reshape(r_dev, lat_dev, nlon)
    loaded = source + coupling * potential
    field, mem = sweeps(3, field, mem, loaded, stiff, decay)
    return tuple(x.transpose(1, 0, 2) for x in (field, mem, potential))


def solution(mesh):
    placed = (
        P("lat", "rad", None),
        P("lat", "rad", None),
        P("lat", None),
        P("lat", "rad"),
        P(),
        P(),
        P(),
        P("lat", "rad", None),
    )
    return jax.shard_map(
        per_device,
        mesh=mesh,
        in_specs=placed,
        out_specs=(P("lat", "rad", None), P("lat", "rad", None), P("lat", "rad", None)),
        check_vma=False,
    )
```

```python
import jax
import jax.numpy as jnp
import numpy as np
from jax import lax
from jax.experimental import pallas as pl
from jax.experimental.pallas import tpu as pltpu
from jax.sharding import PartitionSpec as P

MODES = 256


load_scale = 0.5
kappa_shift = 0.5
relax_factor = 0.8
coupling = 2.0
HIGH = lax.Precision.HIGH


def lookup(material, table):
    onehot = (
        material[:, :, None] == jnp.arange(table.shape[0], dtype=jnp.int32)[None, None, :]
    ).astype(jnp.float32)
    return jnp.sum(onehot * table[None, None, :], axis=-1)


def fourier_parts(nlon, modes, minor=128):
    order = np.arange(modes)
    parts = []
    for place in (np.arange(nlon // minor) * minor, np.arange(minor)):
        angle = (place[:, None] * order[None, :] % nlon) * (2.0 * np.pi / nlon)
        parts += [np.cos(angle), np.sin(angle)]
    scale = np.sqrt(2.0 / nlon)
    return [(part * f).astype(np.float32) for part, f in zip(parts, (scale, scale, 1.0, 1.0))]


def fourier_table(nlon, modes):
    ca, sa, cb, sb = lax.optimization_barrier([jnp.asarray(p) for p in fourier_parts(nlon, modes)])
    ca, sa, cb, sb = ca[:, None], sa[:, None], cb[None], sb[None]
    cos = (ca * cb - sa * sb).reshape(nlon, modes)
    sin = (sa * cb + ca * sb).reshape(nlon, modes)
    return jnp.concatenate([cos, sin], axis=1)


def legendre(lat, degrees):
    theta = np.pi * (np.arange(lat) + 0.5) / lat
    cosine = np.cos(theta)
    before, current, rows = np.zeros(lat), np.ones(lat), []
    for n in range(degrees):
        rows.append(current * np.sqrt(n + 0.5))
        before, current = current, ((2.0 * n + 1.0) * cosine * current - n * before) / (n + 1.0)
    basis = np.stack(rows)
    weighted = basis * (np.pi / lat * np.sin(theta))[None, :]
    return basis, weighted


def sweeps_kernel(steps, gather, *refs):
    if gather:
        f_ref, m_ref, s_ref, stiff_ref, decay_ref, g_ref, f_out, m_out, g_out, *refs = refs
        f_buf, face, lat_in, rad_in, send, recv, g_in, g_send, g_recv = refs
    else:
        f_ref, m_ref, s_ref, stiff_ref, decay_ref, f_out, m_out, *refs = refs
        f_buf, face, lat_in, rad_in, send, recv = refs
    layers, rows, nlon = f_ref.shape
    lat_n, rad_n = lax.axis_size("lat"), lax.axis_size("rad")
    lat, rad = lax.axis_index("lat"), lax.axis_index("rad")
    north = (lax.rem(lat + lat_n - 1, lat_n), rad)
    south = (lax.rem(lat + 1, lat_n), rad)
    below = (lat, lax.rem(rad + rad_n - 1, rad_n))
    above = (lat, lax.rem(rad + 1, rad_n))
    if gather:
        peers = [(lax.rem(lat + d, lat_n), rad) for d in range(1, lat_n)] + [below, above]
    else:
        peers = [north, south, below, above]
    barrier = pltpu.get_barrier_semaphore()
    for peer in peers:
        pl.semaphore_signal(barrier, inc=1, device_id=peer, device_id_type=pl.DeviceIdType.MESH)
    pl.semaphore_wait(barrier, len(peers))

    def remote(src, dst, send_sem, recv_sem, peer):
        copy = pltpu.make_async_remote_copy(
            src_ref=src, dst_ref=dst, send_sem=send_sem, recv_sem=recv_sem,
            device_id=peer, device_id_type=pl.DeviceIdType.MESH,
        )
        copy.start()
        return copy

    weight = relax_factor / (6.0 + kappa_shift)
    w_north = jnp.where(lat > 0, weight, 0.0)
    w_south = jnp.where(lat < lat_n - 1, weight, 0.0)
    w_below = jnp.where(rad > 0, weight, 0.0)
    w_above = jnp.where(rad < rad_n - 1, weight, 0.0)
    row = lax.broadcasted_iota(jnp.int32, (rows, nlon), 0)
    gathered = []
    for step in range(steps):
        old = f_ref if step == 0 else f_buf.at[step - 1]
        new = f_out if step == steps - 1 else f_buf.at[step]
        old_m = m_ref if step == 0 else m_out
        for r in range(layers):
            face[step, 0, r : r + 1, :] = old[r, 0:1, :]
            face[step, 1, r : r + 1, :] = old[r, rows - 1 : rows, :]
        copies = [
            remote(old.at[0], rad_in.at[step, 1], send.at[step, 0], recv.at[step, 0], below),
            remote(old.at[layers - 1], rad_in.at[step, 0], send.at[step, 1], recv.at[step, 1], above),
            remote(face.at[step, 0], lat_in.at[step, 1], send.at[step, 2], recv.at[step, 2], north),
            remote(face.at[step, 1], lat_in.at[step, 0], send.at[step, 3], recv.at[step, 3], south),
        ]
        if gather and step == 0:
            gathered = [
                remote(g_ref, g_in.at[lat], g_send.at[d], g_recv.at[d], peers[d - 1])
                for d in range(1, lat_n)
            ]
        for r in range(layers):
            f, m = old[r], old_m[r]
            beside = pltpu.roll(f, 1, 1) + pltpu.roll(f, nlon - 1, 1)
            beside += jnp.where(row == 0, 0.0, pltpu.roll(f, 1, 0))
            beside += jnp.where(row == rows - 1, 0.0, pltpu.roll(f, rows - 1, 0))
            if r > 0:
                beside += old[r - 1]
            if r < layers - 1:
                beside += old[r + 1]
            stiff = stiff_ref[r]
            update = (s_ref[r] - m) * (weight / stiff) - relax_factor * f + weight * beside
            new[r] = f + update
            m_out[r] = decay_ref[r] * m + stiff * update
        for copy in copies:
            copy.wait()
        for r, slot, w in ((0, 0, w_below), (layers - 1, 1, w_above)):
            extra = w * rad_in[step, slot]
            new[r] += extra
            m_out[r] += stiff_ref[r] * extra
        for r in range(layers):
            for j, slot, w in ((0, 0, w_north), (rows - 1, 1, w_south)):
                extra = w * lat_in[step, slot, r : r + 1, :]
                new[r, j : j + 1, :] += extra
                m_out[r, j : j + 1, :] += stiff_ref[r, j : j + 1, :] * extra
    if gather:
        for copy in gathered:
            copy.wait()
        g_in[lat] = g_ref[...]
        g_out[...] = g_in[...]


def sweeps(steps, field, memory, source, stiff, decay, gravity=None):
    gather = gravity is not None
    layers, rows, nlon = field.shape
    block = jax.ShapeDtypeStruct(field.shape, jnp.float32)
    operands, out = [field, memory, source, stiff, decay], [block, block]
    dma, f32 = pltpu.SemaphoreType.DMA, jnp.float32
    scratch = [
        pltpu.VMEM((steps - 1, layers, rows, nlon), f32),
        pltpu.VMEM((steps, 2, layers, nlon), f32),
        pltpu.VMEM((steps, 2, layers, nlon), f32),
        pltpu.VMEM((steps, 2, rows, nlon), f32),
        dma((steps, 4)),
        dma((steps, 4)),
    ]
    if gather:
        lat_n = lax.axis_size("lat")
        every = (lat_n,) + gravity.shape
        operands.append(gravity)
        out.append(jax.ShapeDtypeStruct(every, f32))
        scratch += [pltpu.VMEM(every, f32), dma((lat_n,)), dma((lat_n,))]
    vmem = pl.BlockSpec(memory_space=pltpu.VMEM)

    def kernel(*refs):
        sweeps_kernel(steps, gather, *refs)

    return pl.pallas_call(
        kernel,
        out_shape=out,
        in_specs=[vmem] * len(operands),
        out_specs=[vmem] * len(out),
        scratch_shapes=scratch,
        compiler_params=pltpu.CompilerParams(
            collective_id=0 if gather else 1, has_side_effects=True
        ),
    )(*operands)


LANES = 128
CHUNKS = 4
SWEEPS = 3


def split_np(x):
    x = np.asarray(x, np.float32)
    hi = x.astype(jnp.bfloat16)
    return hi, (x - hi.astype(np.float32)).astype(jnp.bfloat16)


def split(x):
    hi = x.astype(jnp.bfloat16)
    return hi, (x - hi.astype(jnp.float32)).astype(jnp.bfloat16)


def dot3(left, right, transposed=False):
    dims = (((1,), (1 if transposed else 0,)), ((), ()))

    def one(a, b):
        return lax.dot_general(a, b, dims, preferred_element_type=jnp.float32)

    return one(left[0], right[0]) + (one(left[0], right[1]) + one(left[1], right[0]))


def radix_tables(nlon, modes):
    quarter, per = nlon // 4, modes // 4
    place = np.arange(quarter)[:, None]

    def waves(k):
        order = k + 4 * np.arange(per)[None, :]
        angle = (place * order % nlon) * (2.0 * np.pi / nlon)
        return np.sqrt(2.0 / nlon) * np.cos(angle), np.sqrt(2.0 / nlon) * np.sin(angle)

    (c0, s0), (c1, s1), (c2, s2), (c3, s3) = (waves(k) for k in range(4))
    even = np.concatenate([c0, s0, c2, s2], axis=1)
    odd = np.concatenate(
        [np.concatenate([c1, s1, c3, s3], axis=1), np.concatenate([-s1, c1, s3, -c3], axis=1)],
        axis=0,
    )
    return even, odd


def column_orders(modes):
    per = np.arange(modes // 4)
    return np.concatenate([k + 4 * per for k in (0, 0, 2, 2, 1, 1, 3, 3)])


def swap_groups(parts, width):
    parts, step = list(parts), 1
    lane = lax.broadcasted_iota(jnp.int32, parts[0].shape, 1)
    while step < len(parts):
        low = (lane // (width * step)) % 2 == 0
        for g in range(len(parts)):
            if (g // step) % 2 == 0:
                a, b = parts[g], parts[g + step]
                parts[g] = jnp.where(low, a, pltpu.roll(b, width * step, 1))
                parts[g + step] = jnp.where(low, pltpu.roll(a, LANES - width * step, 1), b)
        step *= 2
    return parts


def fused_kernel(
    u_ref, m_ref, ice_hbm, table_hbm, stiff_ref, decay_ref, mat_ref, grav_ref,
    shift_ref, mu_ref, dec_ref, con_ref,
    u_out, m_out, p_out,
    ice_ref, even_hi, even_lo, odd_hi, odd_lo, expand_ref, fwd_hi, fwd_lo, inv_hi, inv_lo, load_sem,
    ubuf, sbuf, x_in, lat_out, lat_in, g_in, mat_in, pack_out, pack_in, ice_out, ice_in,
    back_out, back_in, gexp, par,
    x_send, x_recv, l_send, l_recv, g_send, g_recv, t_send, t_recv,
    a_send, a_recv, i_send, i_recv, b_send, b_recv,
):
    f32 = jnp.float32
    rows, layers, nlon = u_ref.shape
    lat_n, rad_n = lax.axis_size("lat"), lax.axis_size("rad")
    lat, rad = lax.axis_index("lat"), lax.axis_index("rad")
    count = lat_n * rad_n
    me = lat * rad_n + rad
    total_lat, total_rad = lat_n * rows, rad_n * layers
    halves = rows // 8
    width = LANES // (halves * layers)
    tiles = count * width // LANES
    per_tile = LANES // width
    chunk = nlon // CHUNKS
    last = 2 * SWEEPS
    weight = relax_factor / (6.0 + kappa_shift)

    def device(index):
        return (index // rad_n, lax.rem(index, rad_n))

    def peer(d):
        return lax.rem(me + d, count)

    barrier = pltpu.get_barrier_semaphore()

    def greet(d, carry):
        pl.semaphore_signal(
            barrier, inc=1, device_id=device(peer(d)), device_id_type=pl.DeviceIdType.MESH
        )
        return carry

    lax.fori_loop(1, count, greet, 0)

    pairs = [(u_ref.at[:, r, :], ubuf.at[0, r]) for r in range(layers)]
    pairs += [(m_ref.at[:, r, :], m_out.at[r]) for r in range(layers)]
    pairs.append((ice_hbm, ice_ref))
    at = 0
    for held in (even_hi, even_lo, odd_hi, odd_lo, expand_ref, fwd_hi, fwd_lo, inv_hi, inv_lo):
        pairs.append((table_hbm.at[pl.ds(at, held.shape[0])], held))
        at += held.shape[0]
    loads = [pltpu.make_async_copy(a, b, load_sem.at[n]) for n, (a, b) in enumerate(pairs)]
    for load in loads:
        load.start()
    first = 2 * layers + 1

    def remote(src, dst, send_sem, recv_sem, target):
        return pltpu.make_async_remote_copy(
            src_ref=src, dst_ref=dst, send_sem=send_sem, recv_sem=recv_sem,
            device_id=target, device_id_type=pl.DeviceIdType.MESH,
        )

    def to_all(src_of, dst, send_sem, recv_sem):
        def start(d, carry):
            q = peer(d)
            remote(src_of(q), dst.at[me], send_sem.at[d], recv_sem.at[d], device(q)).start()
            return carry

        lax.fori_loop(1, count, start, 0)

    def each(src_of, dst, send_sem, recv_sem, how):
        def wait(d, carry):
            q = peer(d)
            copy = remote(src_of(q), dst.at[me], send_sem.at[d], recv_sem.at[d], device(q))
            copy.wait_recv() if how == "recv" else copy.wait_send()
            return carry

        lax.fori_loop(1, count, wait, 0)

    sides = (
        (0, rad > 0, 0, (lat, jnp.maximum(rad - 1, 0))),
        (1, rad < rad_n - 1, layers - 1, (lat, jnp.minimum(rad + 1, rad_n - 1))),
    )

    def x_copy(s, side, k, r, target):
        cols = pl.ds(k * chunk, chunk)
        return remote(
            ubuf.at[s, r, :, cols], x_in.at[s, 1 - side, :, cols],
            x_send.at[s, side, k], x_recv.at[s, 1 - side, k], target,
        )

    poles = (
        (0, lat > 0, 0, (jnp.maximum(lat - 1, 0), rad)),
        (1, lat < lat_n - 1, rows - 1, (jnp.minimum(lat + 1, lat_n - 1), rad)),
    )

    def lat_copy(s, side, r, target):
        return remote(
            lat_out.at[s, side, r], lat_in.at[s, 1 - side, r],
            l_send.at[s, side, r], l_recv.at[s, 1 - side, r], target,
        )

    def send_lat(s, r):
        for side, there, j, target in poles:
            @pl.when(there)
            def _():
                lat_out[s, side, r] = ubuf[s, r, j : j + 1, :]
                lat_copy(s, side, r, target).start()

    def sweep(s, more):
        row = lax.broadcasted_iota(jnp.int32, (rows, nlon), 0)

        def forward(r, when):
            @pl.when(jnp.logical_and(when, more))
            def _():
                send_lat(s + 1, r)

        def inner(r):
            for side, there, _, target in poles:
                @pl.when(there)
                def _():
                    lat_copy(s, 1 - side, r, target).wait_recv()

            f, m = ubuf[s, r], m_out[r]
            beside = pltpu.roll(f, 1, 1) + pltpu.roll(f, nlon - 1, 1)
            beside += jnp.where(row == 0, lat_in[s, 0, r], pltpu.roll(f, 1, 0))
            beside += jnp.where(row == rows - 1, lat_in[s, 1, r], pltpu.roll(f, rows - 1, 0))
            if r > 0:
                beside += ubuf[s, r - 1]
            if r < layers - 1:
                beside += ubuf[s, r + 1]
            stiff = stiff_ref[r]
            update = (sbuf[r] - m) * (weight / stiff) - relax_factor * f + weight * beside
            ubuf[s + 1, r] = f + update
            m_out[r] = decay_ref[r] * m + stiff * update
            alone = True
            for side, there, edge, _ in sides:
                if edge == r:
                    alone = jnp.logical_not(there)
            forward(r, alone)

        rest = list(range(1, layers - 1))
        inner(layers - 1)
        inner(0)
        for k in range(CHUNKS):
            for side, there, r, target in sides:
                @pl.when(there)
                def _():
                    cols = slice(k * chunk, (k + 1) * chunk)
                    x_copy(s, 1 - side, k, r, target).wait_recv()
                    extra = weight * x_in[s, side, :, cols]
                    ubuf[s + 1, r, :, cols] += extra
                    m_out[r, :, cols] += stiff_ref[r] * extra
                    if more is True:
                        x_copy(s + 1, side, k, r, target).start()
                    else:
                        @pl.when(more)
                        def _():
                            x_copy(s + 1, side, k, r, target).start()
            if k < len(rest):
                inner(rest[k])

        for side, there, r, _ in sides:
            forward(r, there)

    for side, there, _, _ in poles:
        @pl.when(jnp.logical_not(there))
        def _():
            for s in range(last):
                lat_in[s, side] = jnp.zeros(lat_in.shape[2:], f32)
    g_in[me] = grav_ref[...]
    mat_in[me] = mat_ref[...]
    for load in loads[:first]:
        load.wait()
    ice = ice_ref[...].astype(f32)
    for r in range(layers):
        pos = (rad * layers + (r + 1)).astype(f32) / total_rad
        sbuf[r] = (load_scale * pos) * ice
    for load in loads[first:]:
        load.wait()

    quarter = nlon // 4
    block = layers * rows

    def piece(a):
        cols = slice(a * quarter, (a + 1) * quarter)
        return jnp.concatenate(
            [
                ubuf[0, :, :, cols].reshape(block, quarter),
                m_out[:, :, cols].reshape(block, quarter),
                ice_ref[:, cols].astype(f32),
            ],
            axis=0,
        )

    x0, x1, x2, x3 = (piece(a) for a in range(4))
    half = even_hi.shape[1] // 2
    both, diff = x0 + x2, x1 + x3
    odd = split(jnp.concatenate([x0 - x2, x1 - x3], axis=1))
    spectra = jnp.concatenate(
        [
            dot3(split(both + diff), (even_hi[:, :half], even_lo[:, :half])),
            dot3(split(both - diff), (even_hi[:, half:], even_lo[:, half:])),
            dot3(odd, (odd_hi[...], odd_lo[...])),
        ],
        axis=1,
    )

    pl.semaphore_wait(barrier, count - 1)
    for k in range(CHUNKS):
        for side, there, r, target in sides:
            @pl.when(there)
            def _():
                x_copy(0, side, k, r, target).start()
    for r in range(layers):
        send_lat(0, r)
    to_all(lambda q: grav_ref, g_in, g_send, g_recv)
    to_all(lambda q: mat_ref, mat_in, t_send, t_recv)

    parts = []
    for h in range(halves):
        for r in range(layers):
            at = r * rows + 8 * h
            parts.append(
                jnp.concatenate(
                    [
                        spectra[o + at : o + at + 8, t * LANES : (t + 1) * LANES]
                        for t in range(tiles)
                        for o in (0, block)
                    ],
                    axis=0,
                )
            )
    for p, part in enumerate(swap_groups(parts, width)):
        for t in range(tiles):
            pack_out[per_tile * t + p] = part[16 * t : 16 * (t + 1)]
    to_all(lambda q: pack_out.at[q], pack_in, a_send, a_recv)
    pack_in[me] = pack_out[me]

    sub8 = lax.broadcasted_iota(jnp.int32, (8, LANES), 0)
    group8 = lax.broadcasted_iota(jnp.int32, (8, LANES), 1) // width
    for t in range(tiles):
        cols = slice(t * LANES, (t + 1) * LANES)
        x = spectra[2 * block : 2 * block + 8, cols]
        for h in range(1, halves):
            at = 2 * block + 8 * h
            x = jnp.where(rad == h, spectra[at : at + 8, cols], x)
        for step in (1, 2, 4):
            sb, gb = (sub8 // step) % 2, (group8 // step) % 2
            up = pltpu.roll(pltpu.roll(x, 8 - step, 0), width * step, 1)
            down = pltpu.roll(pltpu.roll(x, step, 0), LANES - width * step, 1)
            x = jnp.where(sb == gb, x, jnp.where(gb == 1, up, down))
        for p in range(per_tile):
            ice_out[per_tile * t + p] = x[p : p + 1]
    to_all(lambda q: ice_out.at[q], ice_in, i_send, i_recv)
    ice_in[me] = ice_out[me]

    each(lambda q: grav_ref, g_in, g_send, g_recv, "recv")
    each(lambda q: mat_ref, mat_in, t_send, t_recv, "recv")
    degrees = fwd_hi.shape[0]
    lane = lax.broadcasted_iota(jnp.int32, (degrees, LANES), 1)
    srow = lax.broadcasted_iota(jnp.int32, (degrees, LANES), 0)
    held = LANES // (layers * total_rad)
    cut = lane // (layers * total_rad) == lax.rem(srow, held)
    lines = degrees // held
    repeat = jnp.where(
        lax.broadcasted_iota(jnp.int32, (degrees, lines), 0) // held
        == lax.broadcasted_iota(jnp.int32, (degrees, lines), 1),
        1.0, 0.0,
    ).astype(jnp.bfloat16)
    wide = []
    for x in range(rad_n):
        lines = split(
            jnp.concatenate([g_in[rad_n * i + x] for i in range(lat_n)], axis=0)
        )
        full = jnp.dot(repeat, lines[0], preferred_element_type=f32) + jnp.dot(
            repeat, lines[1], preferred_element_type=f32
        )
        wide.append(jnp.where(cut, full, 0.0))
    wide = split(jnp.concatenate(wide, axis=1))
    for d in range(total_rad):
        cols = slice(d * LANES, (d + 1) * LANES)
        at = (d // 2) * wide[0].shape[1]
        place = expand_ref[at : at + wide[0].shape[1], (d % 2) * LANES : (d % 2 + 1) * LANES]
        gexp[:, cols] = jnp.dot(wide[0], place, preferred_element_type=f32) + jnp.dot(
            wide[1], place, preferred_element_type=f32
        )

    jrow = lax.broadcasted_iota(jnp.int32, (rows, LANES), 0)
    jlane = (lax.broadcasted_iota(jnp.int32, (rows, LANES), 1) // layers) % rows
    ids = []
    for i in range(lat_n):
        line = mat_in[rad_n * i]
        for x in range(1, rad_n):
            line = line + mat_in[rad_n * i + x]
        ids.append(jnp.where(jrow == jlane, jnp.broadcast_to(line, (rows, LANES)), 0.0))
    source_layer = lax.broadcasted_iota(jnp.int32, (LANES, LANES), 0)
    source_layer = source_layer // block * layers + lax.rem(source_layer, layers)
    spread = jnp.where(
        source_layer == lax.broadcasted_iota(jnp.int32, (LANES, LANES), 1) // width, 1.0, 0.0
    ).astype(jnp.bfloat16)
    ids = jnp.dot(
        jnp.concatenate(ids, axis=0).astype(jnp.bfloat16), spread,
        preferred_element_type=f32,
    )
    for n, table in enumerate((mu_ref, dec_ref, con_ref)):
        value = jnp.zeros((total_lat, LANES), f32)
        for k in range(table.shape[0]):
            value = jnp.where(ids == k, table[k], value)
        par[n] = value

    def two(s, carry):
        sweep(s, True)
        return carry

    lax.fori_loop(0, SWEEPS - 1, two, 0)

    each(lambda q: pack_out.at[q], pack_in, a_send, a_recv, "recv")
    each(lambda q: ice_out.at[q], ice_in, i_send, i_recv, "recv")
    near = lax.broadcasted_iota(jnp.int32, (16, LANES), 1) < LANES // 2
    us, qs, ss = [], [], []
    sub = lax.broadcasted_iota(jnp.int32, (8, LANES), 0)
    for i in range(lat_n):
        a, b = pack_in[rad_n * i], pack_in[rad_n * i + 1]
        top = jnp.where(near, a, pltpu.roll(b, LANES // 2, 1))
        low = jnp.where(near, pltpu.roll(a, LANES // 2, 1), b)
        us += [top[:8], low[:8]]
        qs += [top[8:], low[8:]]
        for x in range(rad_n):
            ss.append(
                jnp.where(sub == group8, jnp.broadcast_to(ice_in[rad_n * i + x], (8, LANES)), 0.0)
            )
    u, q, s_hat = (jnp.concatenate(v, axis=0) for v in (us, qs, ss))
    step = width
    while step < LANES:
        s_hat = s_hat + pltpu.roll(s_hat, step, 1)
        step *= 2
    glane = lax.broadcasted_iota(jnp.int32, (total_lat, LANES), 1)
    grow = lax.broadcasted_iota(jnp.int32, (total_lat, LANES), 0)
    s_hat = s_hat * ((glane // width + 1).astype(f32) * (load_scale / total_rad))
    shift = shift_ref[pl.ds(me, 1), :]
    stiff, decay, contrast = par[0], par[1], par[2]
    scaled = weight / stiff
    for n in range(SWEEPS):
        beside = shift * u
        beside += jnp.where(grow == 0, 0.0, pltpu.roll(u, 1, 0))
        beside += jnp.where(grow == total_lat - 1, 0.0, pltpu.roll(u, total_lat - 1, 0))
        beside += jnp.where(glane < width, 0.0, pltpu.roll(u, width, 1))
        beside += jnp.where(glane >= LANES - width, 0.0, pltpu.roll(u, LANES - width, 1))
        update = (s_hat - q) * scaled - relax_factor * u + weight * beside
        u = u + update
        q = decay * q + stiff * update
    rho = contrast * u
    zero = jnp.logical_and(me == 0, lax.rem(glane, width) == 0)
    mean = jnp.sum(jnp.where(zero, rho, 0.0)) / (total_lat * total_rad)
    rho = rho - jnp.where(zero, mean, 0.0)
    coef = dot3((fwd_hi[...], fwd_lo[...]), split(rho))
    phi = gexp[:, :LANES] * coef
    for d in range(1, total_rad):
        phi += gexp[:, d * LANES : (d + 1) * LANES] * pltpu.roll(coef, width * d, 1)
    synth = dot3((inv_hi[...], inv_lo[...]), split(phi))
    near8 = lax.broadcasted_iota(jnp.int32, (8, LANES), 1) < LANES // 2
    for i in range(lat_n):
        a, b = synth[rows * i : rows * i + 8], synth[rows * i + 8 : rows * i + 16]
        back_out[rad_n * i] = jnp.where(near8, a, pltpu.roll(b, LANES // 2, 1))
        back_out[rad_n * i + 1] = jnp.where(near8, pltpu.roll(a, LANES // 2, 1), b)
    to_all(lambda q: back_out.at[q], back_in, b_send, b_recv)
    back_in[me] = back_out[me]

    sweep(SWEEPS - 1, True)

    each(lambda q: back_out.at[q], back_in, b_send, b_recv, "recv")
    parts = swap_groups(
        [
            jnp.concatenate([back_in[per_tile * t + p] for t in range(tiles)], axis=0)
            for p in range(per_tile)
        ],
        width,
    )
    lines = []
    for r in range(layers):
        for h in range(halves):
            part = parts[h * layers + r]
            lines.append(
                jnp.concatenate([part[8 * t : 8 * (t + 1)] for t in range(tiles)], axis=1)
            )
    z = jnp.concatenate(lines, axis=0)
    y0 = dot3(split(z[:, :half]), (even_hi[:, :half], even_lo[:, :half]), True)
    y2 = dot3(split(z[:, half : 2 * half]), (even_hi[:, half:], even_lo[:, half:]), True)
    y13 = dot3(split(z[:, 2 * half :]), (odd_hi[...], odd_lo[...]), True)
    alpha, beta = y13[:, :quarter], y13[:, quarter:]
    plus, minus = y0 + y2, y0 - y2
    for a, value in enumerate((plus + alpha, minus + beta, plus - alpha, minus - beta)):
        cols = slice(a * quarter, (a + 1) * quarter)
        value = value.reshape(layers, rows, quarter)
        p_out[:, :, cols] = value
        sbuf[:, :, cols] += coupling * value

    def rest(s, carry):
        sweep(s, s + 1 < last)
        return carry

    lax.fori_loop(SWEEPS, last, rest, 0)
    u_out[...] = ubuf[last]

    each(lambda q: grav_ref, g_in, g_send, g_recv, "send")
    each(lambda q: mat_ref, mat_in, t_send, t_recv, "send")
    each(lambda q: pack_out.at[q], pack_in, a_send, a_recv, "send")
    each(lambda q: ice_out.at[q], ice_in, i_send, i_recv, "send")
    each(lambda q: back_out.at[q], back_in, b_send, b_recv, "send")

    def drain(s, carry):
        for side, there, r, target in sides:
            @pl.when(there)
            def _():
                for k in range(CHUNKS):
                    x_copy(s, side, k, r, target).wait_send()
        for side, there, _, target in poles:
            @pl.when(there)
            def _():
                for r in range(layers):
                    lat_copy(s, side, r, target).wait_send()
        return carry

    lax.fori_loop(0, last, drain, 0)


def deliver_kernel(*refs):
    count = (len(refs) - 1) // 2
    sem = refs[-1]
    copies = []
    for n in range(count):
        for r in range(refs[n].shape[0]):
            copies.append(
                pltpu.make_async_copy(refs[n].at[r], refs[count + n].at[:, r, :], sem.at[n, r])
            )
    for copy in copies:
        copy.start()
    for copy in copies:
        copy.wait()


def deliver(blocks):
    layers, rows, nlon = blocks[0].shape
    return tuple(
        pl.pallas_call(
            deliver_kernel,
            out_shape=[jax.ShapeDtypeStruct((rows, layers, nlon), jnp.float32)] * len(blocks),
            in_specs=[pl.BlockSpec(memory_space=pltpu.VMEM)] * len(blocks),
            out_specs=[pl.BlockSpec(memory_space=pltpu.HBM)] * len(blocks),
            scratch_shapes=[pltpu.SemaphoreType.DMA((len(blocks), layers))],
            compiler_params=pltpu.CompilerParams(vmem_limit_bytes=4 << 20),
        )(*blocks)
    )


def fused(displacement, memory, ice_class, stiff, decay, material, tables, gravity):
    lat_dev, r_dev, nlon = displacement.shape
    lat_n, rad_n = lax.axis_size("lat"), lax.axis_size("rad")
    count, total_lat, total_rad = lat_n * rad_n, lat_n * lat_dev, rad_n * r_dev
    degrees = gravity.shape[0] * lat_n
    width = 2 * MODES // count
    bf16, f32 = jnp.bfloat16, jnp.float32
    even, odd = (split_np(t) for t in radix_tables(nlon, MODES))
    basis, weighted = legendre(total_lat, degrees)
    fwd, inv = split_np(weighted), split_np(basis.T)
    orders = column_orders(MODES).reshape(count, width)
    shift = np.tile(2.0 * np.cos(2.0 * np.pi * orders / nlon), (1, total_rad)).astype(np.float32)
    held = LANES // (r_dev * total_rad)
    expand = np.zeros((rad_n, held, r_dev, total_rad, total_rad, total_rad, width))
    for x in range(rad_n):
        for r in range(r_dev):
            for d in range(total_rad):
                to = x * r_dev + r
                expand[x, :, r, (to - d) % total_rad, d, to, :] = 1.0
    expand = expand.reshape(rad_n * LANES, total_rad // 2, 2 * LANES)
    expand = expand.transpose(1, 0, 2).reshape(-1, 2 * LANES).astype(bf16)
    tabs = [*even, *odd, expand, *fwd, *inv]
    rad = lax.axis_index("rad")
    ids = material.astype(f32).reshape(1, lat_dev * r_dev)
    ids = jnp.concatenate([jnp.where(rad == x, ids, 0.0) for x in range(rad_n)], axis=1)
    gravity = gravity.reshape(-1, LANES)
    lines = gravity.shape[0]
    operands = [
        displacement, memory, ice_class, np.concatenate(tabs, axis=0),
        stiff, decay, ids, gravity, shift, *tables,
    ]
    operands = [jnp.asarray(x) for x in operands]
    vmem = pl.BlockSpec(memory_space=pltpu.VMEM)
    smem = pl.BlockSpec(memory_space=pltpu.SMEM)
    hbm = pl.BlockSpec(memory_space=pltpu.HBM)
    streamed = 4
    dma = pltpu.SemaphoreType.DMA
    steps = 2 * SWEEPS
    block = jax.ShapeDtypeStruct((r_dev, lat_dev, nlon), f32)
    out = pl.pallas_call(
        fused_kernel,
        out_shape=[block] * 3,
        in_specs=[hbm] * streamed
        + [vmem] * (len(operands) - streamed - len(tables))
        + [smem] * len(tables),
        out_specs=[vmem] * 3,
        scratch_shapes=[pltpu.VMEM(x.shape, x.dtype) for x in (ice_class, *tabs)]
        + [
            dma((2 * r_dev + 1 + len(tabs),)),
            pltpu.VMEM((steps + 1, r_dev, lat_dev, nlon), f32),
            pltpu.VMEM((r_dev, lat_dev, nlon), f32),
            pltpu.VMEM((steps, 2, lat_dev, nlon), f32),
            pltpu.VMEM((steps, 2, r_dev, 1, nlon), f32),
            pltpu.VMEM((steps, 2, r_dev, 1, nlon), f32),
            pltpu.VMEM((count, lines, LANES), f32),
            pltpu.VMEM((count, 1, LANES), f32),
            pltpu.VMEM((count, 16, LANES), f32),
            pltpu.VMEM((count, 16, LANES), f32),
            pltpu.VMEM((count, 1, LANES), f32),
            pltpu.VMEM((count, 1, LANES), f32),
            pltpu.VMEM((count, 8, LANES), f32),
            pltpu.VMEM((count, 8, LANES), f32),
            pltpu.VMEM((degrees, total_rad * LANES), f32),
            pltpu.VMEM((3, total_lat, LANES), f32),
            dma((steps, 2, CHUNKS)), dma((steps, 2, CHUNKS)),
            dma((steps, 2, r_dev)), dma((steps, 2, r_dev)),
        ] + [dma((count,))] * 10,
        compiler_params=pltpu.CompilerParams(
            collective_id=2, has_side_effects=True, vmem_limit_bytes=54500000
        ),
    )(*operands)
    return deliver(out)


def fits(lat_dev, r_dev, total_lat, total_rad, rad_n, count, degrees):
    width = 2 * MODES // count
    return (
        rad_n == 2
        and lat_dev == 16
        and width * count == 2 * MODES
        and width * total_rad == LANES
        and rad_n * lat_dev * r_dev == LANES
        and LANES % (r_dev * total_rad) == 0
        and total_rad % 2 == 0
        and degrees == 2 * LANES
        and total_lat == 2 * LANES
    )


def per_device(
    displacement, memory, ice_class, material, mu_table, decay_table, contrast_table, gravity_kernel
):
    lat_dev, r_dev, nlon = displacement.shape
    lat_count = lax.axis_size("lat")
    rad_count = lax.axis_size("rad")
    rad_index = lax.axis_index("rad")
    total_lat = lat_count * lat_dev
    total_rad = rad_count * r_dev
    degrees = gravity_kernel.shape[0] * lat_count
    cols = 2 * MODES
    columns = cols // lat_count
    stiff = lookup(material.T, mu_table)[:, :, None]
    decay = lookup(material.T, decay_table)[:, :, None]
    contrast = lookup(material.T, contrast_table)[:, :, None]
    layer_pos = (rad_index * r_dev + jnp.arange(r_dev, dtype=jnp.int32) + 1).astype(
        jnp.float32
    ) / total_rad
    source = load_scale * ice_class.astype(jnp.float32)[None, :, :] * layer_pos[:, None, None]
    devices = lat_count * rad_count
    if fits(lat_dev, r_dev, total_lat, total_rad, rad_count, devices, degrees):
        tables = (mu_table, decay_table, contrast_table)
        return fused(
            displacement, memory, ice_class, stiff, decay, material, tables, gravity_kernel
        )
    basis, weighted = legendre(total_lat, degrees)
    projection = jnp.asarray(
        np.concatenate([weighted, np.ones((8, total_lat))]).astype(np.float32)
    )
    weight_sum = jnp.asarray(weighted.sum(axis=1).astype(np.float32))
    basis = jnp.asarray(basis.T.astype(np.float32))
    table = fourier_table(nlon, MODES)
    field, mem, kernel_every = sweeps(
        3,
        displacement.transpose(1, 0, 2),
        memory.transpose(1, 0, 2),
        source,
        stiff,
        decay,
        gravity_kernel.reshape(gravity_kernel.shape[0], -1),
    )
    kernel_every = kernel_every.reshape((degrees,) + gravity_kernel.shape[1:])
    rho = contrast * field
    spectra = jnp.dot(rho.reshape(lat_dev * r_dev, nlon), table, precision=HIGH)
    spread = lax.all_to_all(
        spectra.reshape(r_dev, lat_dev, cols).transpose(1, 0, 2), "lat", split_axis=2, concat_axis=0, tiled=True
    )
    coef_cols = jnp.dot(
        projection, spread.reshape(total_lat, r_dev * columns), precision=HIGH
    ).reshape(degrees + 8, r_dev, columns)
    coef_all = lax.all_gather(coef_cols, "rad", axis=1, tiled=True)
    first_order = (lax.axis_index("lat") * columns + jnp.arange(columns, dtype=jnp.int32)) == 0
    mean_row = jnp.sum(coef_all[degrees], axis=0) / (total_lat * total_rad)
    mean_row = jnp.where(first_order, mean_row, 0.0)
    coef_all = coef_all[:degrees] - weight_sum[:, None, None] * mean_row[None, None, :]
    phi_cols = jnp.sum(kernel_every[:, :, :, None] * coef_all[:, None, :, :], axis=2)
    synth_cols = jnp.dot(
        basis, phi_cols.reshape(degrees, r_dev * columns), precision=HIGH
    ).reshape(total_lat, r_dev, columns)
    synth = lax.all_to_all(synth_cols, "lat", split_axis=0, concat_axis=2, tiled=True)
    potential = lax.dot_general(
        synth.transpose(1, 0, 2).reshape(r_dev * lat_dev, cols), table, (((1,), (1,)), ((), ())), precision=HIGH
    ).reshape(r_dev, lat_dev, nlon)
    loaded = source + coupling * potential
    field, mem = sweeps(3, field, mem, loaded, stiff, decay)
    return tuple(x.transpose(1, 0, 2) for x in (field, mem, potential))


def solution(mesh):
    placed = (
        P("lat", "rad", None),
        P("lat", "rad", None),
        P("lat", None),
        P("lat", "rad"),
        P(),
        P(),
        P(),
        P("lat", "rad", None),
    )
    return jax.shard_map(
        per_device,
        mesh=mesh,
        in_specs=placed,
        out_specs=(P("lat", "rad", None), P("lat", "rad", None), P("lat", "rad", None)),
        check_vma=False,
    )
```

```python
import jax
import jax.numpy as jnp
import numpy as np
from jax import lax
from jax.experimental import pallas as pl
from jax.experimental.pallas import tpu as pltpu
from jax.sharding import PartitionSpec as P

MODES = 256


load_scale = 0.5
kappa_shift = 0.5
relax_factor = 0.8
coupling = 2.0
HIGH = lax.Precision.HIGH


def lookup(material, table):
    onehot = (
        material[:, :, None] == jnp.arange(table.shape[0], dtype=jnp.int32)[None, None, :]
    ).astype(jnp.float32)
    return jnp.sum(onehot * table[None, None, :], axis=-1)


def fourier_parts(nlon, modes, minor=128):
    order = np.arange(modes)
    parts = []
    for place in (np.arange(nlon // minor) * minor, np.arange(minor)):
        angle = (place[:, None] * order[None, :] % nlon) * (2.0 * np.pi / nlon)
        parts += [np.cos(angle), np.sin(angle)]
    scale = np.sqrt(2.0 / nlon)
    return [(part * f).astype(np.float32) for part, f in zip(parts, (scale, scale, 1.0, 1.0))]


def fourier_table(nlon, modes):
    ca, sa, cb, sb = lax.optimization_barrier([jnp.asarray(p) for p in fourier_parts(nlon, modes)])
    ca, sa, cb, sb = ca[:, None], sa[:, None], cb[None], sb[None]
    cos = (ca * cb - sa * sb).reshape(nlon, modes)
    sin = (sa * cb + ca * sb).reshape(nlon, modes)
    return jnp.concatenate([cos, sin], axis=1)


def legendre(lat, degrees):
    theta = np.pi * (np.arange(lat) + 0.5) / lat
    cosine = np.cos(theta)
    before, current, rows = np.zeros(lat), np.ones(lat), []
    for n in range(degrees):
        rows.append(current * np.sqrt(n + 0.5))
        before, current = current, ((2.0 * n + 1.0) * cosine * current - n * before) / (n + 1.0)
    basis = np.stack(rows)
    weighted = basis * (np.pi / lat * np.sin(theta))[None, :]
    return basis, weighted


def sweeps_kernel(steps, gather, *refs):
    if gather:
        f_ref, m_ref, s_ref, stiff_ref, decay_ref, g_ref, f_out, m_out, g_out, *refs = refs
        f_buf, face, lat_in, rad_in, send, recv, g_in, g_send, g_recv = refs
    else:
        f_ref, m_ref, s_ref, stiff_ref, decay_ref, f_out, m_out, *refs = refs
        f_buf, face, lat_in, rad_in, send, recv = refs
    layers, rows, nlon = f_ref.shape
    lat_n, rad_n = lax.axis_size("lat"), lax.axis_size("rad")
    lat, rad = lax.axis_index("lat"), lax.axis_index("rad")
    north = (lax.rem(lat + lat_n - 1, lat_n), rad)
    south = (lax.rem(lat + 1, lat_n), rad)
    below = (lat, lax.rem(rad + rad_n - 1, rad_n))
    above = (lat, lax.rem(rad + 1, rad_n))
    if gather:
        peers = [(lax.rem(lat + d, lat_n), rad) for d in range(1, lat_n)] + [below, above]
    else:
        peers = [north, south, below, above]
    barrier = pltpu.get_barrier_semaphore()
    for peer in peers:
        pl.semaphore_signal(barrier, inc=1, device_id=peer, device_id_type=pl.DeviceIdType.MESH)
    pl.semaphore_wait(barrier, len(peers))

    def remote(src, dst, send_sem, recv_sem, peer):
        copy = pltpu.make_async_remote_copy(
            src_ref=src, dst_ref=dst, send_sem=send_sem, recv_sem=recv_sem,
            device_id=peer, device_id_type=pl.DeviceIdType.MESH,
        )
        copy.start()
        return copy

    weight = relax_factor / (6.0 + kappa_shift)
    w_north = jnp.where(lat > 0, weight, 0.0)
    w_south = jnp.where(lat < lat_n - 1, weight, 0.0)
    w_below = jnp.where(rad > 0, weight, 0.0)
    w_above = jnp.where(rad < rad_n - 1, weight, 0.0)
    row = lax.broadcasted_iota(jnp.int32, (rows, nlon), 0)
    gathered = []
    for step in range(steps):
        old = f_ref if step == 0 else f_buf.at[step - 1]
        new = f_out if step == steps - 1 else f_buf.at[step]
        old_m = m_ref if step == 0 else m_out
        for r in range(layers):
            face[step, 0, r : r + 1, :] = old[r, 0:1, :]
            face[step, 1, r : r + 1, :] = old[r, rows - 1 : rows, :]
        copies = [
            remote(old.at[0], rad_in.at[step, 1], send.at[step, 0], recv.at[step, 0], below),
            remote(old.at[layers - 1], rad_in.at[step, 0], send.at[step, 1], recv.at[step, 1], above),
            remote(face.at[step, 0], lat_in.at[step, 1], send.at[step, 2], recv.at[step, 2], north),
            remote(face.at[step, 1], lat_in.at[step, 0], send.at[step, 3], recv.at[step, 3], south),
        ]
        if gather and step == 0:
            gathered = [
                remote(g_ref, g_in.at[lat], g_send.at[d], g_recv.at[d], peers[d - 1])
                for d in range(1, lat_n)
            ]
        for r in range(layers):
            f, m = old[r], old_m[r]
            beside = pltpu.roll(f, 1, 1) + pltpu.roll(f, nlon - 1, 1)
            beside += jnp.where(row == 0, 0.0, pltpu.roll(f, 1, 0))
            beside += jnp.where(row == rows - 1, 0.0, pltpu.roll(f, rows - 1, 0))
            if r > 0:
                beside += old[r - 1]
            if r < layers - 1:
                beside += old[r + 1]
            stiff = stiff_ref[r]
            update = (s_ref[r] - m) * (weight / stiff) - relax_factor * f + weight * beside
            new[r] = f + update
            m_out[r] = decay_ref[r] * m + stiff * update
        for copy in copies:
            copy.wait()
        for r, slot, w in ((0, 0, w_below), (layers - 1, 1, w_above)):
            extra = w * rad_in[step, slot]
            new[r] += extra
            m_out[r] += stiff_ref[r] * extra
        for r in range(layers):
            for j, slot, w in ((0, 0, w_north), (rows - 1, 1, w_south)):
                extra = w * lat_in[step, slot, r : r + 1, :]
                new[r, j : j + 1, :] += extra
                m_out[r, j : j + 1, :] += stiff_ref[r, j : j + 1, :] * extra
    if gather:
        for copy in gathered:
            copy.wait()
        g_in[lat] = g_ref[...]
        g_out[...] = g_in[...]


def sweeps(steps, field, memory, source, stiff, decay, gravity=None):
    gather = gravity is not None
    layers, rows, nlon = field.shape
    block = jax.ShapeDtypeStruct(field.shape, jnp.float32)
    operands, out = [field, memory, source, stiff, decay], [block, block]
    dma, f32 = pltpu.SemaphoreType.DMA, jnp.float32
    scratch = [
        pltpu.VMEM((steps - 1, layers, rows, nlon), f32),
        pltpu.VMEM((steps, 2, layers, nlon), f32),
        pltpu.VMEM((steps, 2, layers, nlon), f32),
        pltpu.VMEM((steps, 2, rows, nlon), f32),
        dma((steps, 4)),
        dma((steps, 4)),
    ]
    if gather:
        lat_n = lax.axis_size("lat")
        every = (lat_n,) + gravity.shape
        operands.append(gravity)
        out.append(jax.ShapeDtypeStruct(every, f32))
        scratch += [pltpu.VMEM(every, f32), dma((lat_n,)), dma((lat_n,))]
    vmem = pl.BlockSpec(memory_space=pltpu.VMEM)

    def kernel(*refs):
        sweeps_kernel(steps, gather, *refs)

    return pl.pallas_call(
        kernel,
        out_shape=out,
        in_specs=[vmem] * len(operands),
        out_specs=[vmem] * len(out),
        scratch_shapes=scratch,
        compiler_params=pltpu.CompilerParams(
            collective_id=0 if gather else 1, has_side_effects=True
        ),
    )(*operands)


LANES = 128
CHUNKS = 4
SWEEPS = 3


def split_np(x):
    x = np.asarray(x, np.float32)
    hi = x.astype(jnp.bfloat16)
    return hi, (x - hi.astype(np.float32)).astype(jnp.bfloat16)


def split(x):
    hi = x.astype(jnp.bfloat16)
    return hi, (x - hi.astype(jnp.float32)).astype(jnp.bfloat16)


def dot3(left, right, transposed=False):
    dims = (((1,), (1 if transposed else 0,)), ((), ()))

    def one(a, b):
        return lax.dot_general(a, b, dims, preferred_element_type=jnp.float32)

    return one(left[0], right[0]) + (one(left[0], right[1]) + one(left[1], right[0]))


def radix_tables(nlon, modes):
    quarter, per = nlon // 4, modes // 4
    place = np.arange(quarter)[:, None]

    def waves(k):
        order = k + 4 * np.arange(per)[None, :]
        angle = (place * order % nlon) * (2.0 * np.pi / nlon)
        return np.sqrt(2.0 / nlon) * np.cos(angle), np.sqrt(2.0 / nlon) * np.sin(angle)

    (c0, s0), (c1, s1), (c2, s2), (c3, s3) = (waves(k) for k in range(4))
    even = np.concatenate([c0, s0, c2, s2], axis=1)
    odd = np.concatenate(
        [np.concatenate([c1, s1, c3, s3], axis=1), np.concatenate([-s1, c1, s3, -c3], axis=1)],
        axis=0,
    )
    return even, odd


def column_orders(modes):
    per = np.arange(modes // 4)
    return np.concatenate([k + 4 * per for k in (0, 0, 2, 2, 1, 1, 3, 3)])


def swap_groups(parts, width):
    parts, step = list(parts), 1
    lane = lax.broadcasted_iota(jnp.int32, parts[0].shape, 1)
    while step < len(parts):
        low = (lane // (width * step)) % 2 == 0
        for g in range(len(parts)):
            if (g // step) % 2 == 0:
                a, b = parts[g], parts[g + step]
                parts[g] = jnp.where(low, a, pltpu.roll(b, width * step, 1))
                parts[g + step] = jnp.where(low, pltpu.roll(a, LANES - width * step, 1), b)
        step *= 2
    return parts


def fused_kernel(
    u_ref, m_ref, ice_hbm, material_hbm, gravity_hbm, mu_hbm, dec_hbm, con_hbm, shift_hbm, table_hbm,
    u_out, m_out, p_out,
    ice_ref, material, gravity, mu_ref, dec_ref, con_ref, shift_ref, pad,
    stiff_ref, decay_ref, mat_ref, grav_ref,
    even_hi, even_lo, odd_hi, odd_lo, fwd_hi, fwd_lo, inv_hi, inv_lo, load_sem,
    ubuf, sbuf, x_in, lat_out, lat_in, g_in, mat_in, pack_out, pack_in, ice_out, ice_in,
    back_out, back_in, gexp, par,
    x_send, x_recv, l_send, l_recv, g_send, g_recv, t_send, t_recv,
    a_send, a_recv, i_send, i_recv, b_send, b_recv,
):
    f32 = jnp.float32
    rows, layers, nlon = u_ref.shape
    lat_n, rad_n = lax.axis_size("lat"), lax.axis_size("rad")
    lat, rad = lax.axis_index("lat"), lax.axis_index("rad")
    count = lat_n * rad_n
    me = lat * rad_n + rad
    total_lat, total_rad = lat_n * rows, rad_n * layers
    halves = rows // 8
    width = LANES // (halves * layers)
    tiles = count * width // LANES
    per_tile = LANES // width
    chunk = nlon // CHUNKS
    last = 2 * SWEEPS
    weight = relax_factor / (6.0 + kappa_shift)

    def device(index):
        return (index // rad_n, lax.rem(index, rad_n))

    def peer(d):
        return lax.rem(me + d, count)

    barrier = pltpu.get_barrier_semaphore()

    def greet(d, carry):
        pl.semaphore_signal(
            barrier, inc=1, device_id=device(peer(d)), device_id_type=pl.DeviceIdType.MESH
        )
        return carry

    lax.fori_loop(1, count, greet, 0)

    pairs = [(u_ref.at[:, r, :], ubuf.at[0, r]) for r in range(layers)]
    pairs += [(m_ref.at[:, r, :], m_out.at[r]) for r in range(layers)]
    pairs += [
        (ice_hbm, ice_ref), (material_hbm, material), (gravity_hbm, gravity), (mu_hbm, mu_ref),
        (dec_hbm, dec_ref), (con_hbm, con_ref), (shift_hbm, shift_ref),
    ]
    first = len(pairs)
    at = 0
    for held in (even_hi, even_lo, odd_hi, odd_lo, fwd_hi, fwd_lo, inv_hi, inv_lo):
        pairs.append((table_hbm.at[pl.ds(at, held.shape[0])], held))
        at += held.shape[0]
    loads = [pltpu.make_async_copy(a, b, load_sem.at[n]) for n, (a, b) in enumerate(pairs)]
    for load in loads:
        load.start()

    def remote(src, dst, send_sem, recv_sem, target):
        return pltpu.make_async_remote_copy(
            src_ref=src, dst_ref=dst, send_sem=send_sem, recv_sem=recv_sem,
            device_id=target, device_id_type=pl.DeviceIdType.MESH,
        )

    def to_all(src_of, dst, send_sem, recv_sem):
        def start(d, carry):
            q = peer(d)
            remote(src_of(q), dst.at[me], send_sem.at[d], recv_sem.at[d], device(q)).start()
            return carry

        lax.fori_loop(1, count, start, 0)

    def each(src_of, dst, send_sem, recv_sem, how):
        def wait(d, carry):
            q = peer(d)
            copy = remote(src_of(q), dst.at[me], send_sem.at[d], recv_sem.at[d], device(q))
            copy.wait_recv() if how == "recv" else copy.wait_send()
            return carry

        lax.fori_loop(1, count, wait, 0)

    sides = (
        (0, rad > 0, 0, (lat, jnp.maximum(rad - 1, 0))),
        (1, rad < rad_n - 1, layers - 1, (lat, jnp.minimum(rad + 1, rad_n - 1))),
    )

    def x_copy(s, side, k, r, target):
        cols = pl.ds(k * chunk, chunk)
        return remote(
            ubuf.at[s, r, :, cols], x_in.at[s, 1 - side, :, cols],
            x_send.at[s, side, k], x_recv.at[s, 1 - side, k], target,
        )

    poles = (
        (0, lat > 0, 0, (jnp.maximum(lat - 1, 0), rad)),
        (1, lat < lat_n - 1, rows - 1, (jnp.minimum(lat + 1, lat_n - 1), rad)),
    )

    def lat_copy(s, side, r, target):
        return remote(
            lat_out.at[s, side, r], lat_in.at[s, 1 - side, r],
            l_send.at[s, side, r], l_recv.at[s, 1 - side, r], target,
        )

    def send_lat(s, r):
        for side, there, j, target in poles:
            @pl.when(there)
            def _():
                lat_out[s, side, r] = ubuf[s, r, j : j + 1, :]
                lat_copy(s, side, r, target).start()

    def sweep(s, more):
        row = lax.broadcasted_iota(jnp.int32, (rows, nlon), 0)

        def forward(r, when):
            @pl.when(jnp.logical_and(when, more))
            def _():
                send_lat(s + 1, r)

        def inner(r):
            for side, there, _, target in poles:
                @pl.when(there)
                def _():
                    lat_copy(s, 1 - side, r, target).wait_recv()

            f, m = ubuf[s, r], m_out[r]
            beside = pltpu.roll(f, 1, 1) + pltpu.roll(f, nlon - 1, 1)
            beside += jnp.where(row == 0, lat_in[s, 0, r], pltpu.roll(f, 1, 0))
            beside += jnp.where(row == rows - 1, lat_in[s, 1, r], pltpu.roll(f, rows - 1, 0))
            if r > 0:
                beside += ubuf[s, r - 1]
            if r < layers - 1:
                beside += ubuf[s, r + 1]
            stiff = stiff_ref[r]
            update = (sbuf[r] - m) * (weight / stiff) - relax_factor * f + weight * beside
            ubuf[s + 1, r] = f + update
            m_out[r] = decay_ref[r] * m + stiff * update
            alone = True
            for side, there, edge, _ in sides:
                if edge == r:
                    alone = jnp.logical_not(there)
            forward(r, alone)

        rest = list(range(1, layers - 1))
        inner(layers - 1)
        inner(0)
        for k in range(CHUNKS):
            for side, there, r, target in sides:
                @pl.when(there)
                def _():
                    cols = slice(k * chunk, (k + 1) * chunk)
                    x_copy(s, 1 - side, k, r, target).wait_recv()
                    extra = weight * x_in[s, side, :, cols]
                    ubuf[s + 1, r, :, cols] += extra
                    m_out[r, :, cols] += stiff_ref[r] * extra
                    if more is True:
                        x_copy(s + 1, side, k, r, target).start()
                    else:
                        @pl.when(more)
                        def _():
                            x_copy(s + 1, side, k, r, target).start()
            if k < len(rest):
                inner(rest[k])

        for side, there, r, _ in sides:
            forward(r, there)

    for side, there, _, _ in poles:
        @pl.when(jnp.logical_not(there))
        def _():
            for s in range(last):
                lat_in[s, side] = jnp.zeros(lat_in.shape[2:], f32)
    for load in loads[:first]:
        load.wait()
    pad[...] = jnp.zeros_like(pad)
    pad[0, :layers, :rows] = material[...].astype(f32)
    own = gravity.shape[2]
    for r in range(layers):
        pad[1 + r, :, :own] = gravity[r]
    prow = lax.broadcasted_iota(jnp.int32, (rows, LANES), 0)
    plane = lax.broadcasted_iota(jnp.int32, (rows, LANES), 1)
    line = jnp.zeros((1, LANES), f32)
    for r in range(layers):
        kind = pad[0, r : r + 1]
        for x in range(rad_n):
            at = (x * layers + r) * rows
            line += jnp.where(rad == x, pltpu.roll(kind, at, 1) if at else kind, 0.0)
        column = jnp.sum(jnp.where(prow == plane, kind, 0.0), axis=1, keepdims=True)
        for table, held in ((mu_ref, stiff_ref), (dec_ref, decay_ref)):
            value = jnp.zeros((rows, 1), f32)
            for k in range(table.shape[0]):
                value = jnp.where(column == k, table[k], value)
            held[r] = value
        full = pad[1 + r]
        step = own
        while step < LANES:
            full = full + pltpu.roll(full, step, 1)
            step *= 2
        keep = lax.broadcasted_iota(jnp.int32, full.shape, 1) // own == lax.broadcasted_iota(
            jnp.int32, full.shape, 0
        )
        grav_ref[r : r + 1] = jnp.sum(jnp.where(keep, full, 0.0), axis=0, keepdims=True)
    mat_ref[...] = line
    g_in[me] = grav_ref[...]
    mat_in[me] = mat_ref[...]
    ice = ice_ref[...].astype(f32)
    for r in range(layers):
        pos = (rad * layers + (r + 1)).astype(f32) / total_rad
        sbuf[r] = (load_scale * pos) * ice
    for load in loads[first:]:
        load.wait()

    quarter = nlon // 4
    block = layers * rows

    def piece(a):
        cols = slice(a * quarter, (a + 1) * quarter)
        return jnp.concatenate(
            [
                ubuf[0, :, :, cols].reshape(block, quarter),
                m_out[:, :, cols].reshape(block, quarter),
                ice_ref[:, cols].astype(f32),
            ],
            axis=0,
        )

    x0, x1, x2, x3 = (piece(a) for a in range(4))
    half = even_hi.shape[1] // 2
    both, diff = x0 + x2, x1 + x3
    odd = split(jnp.concatenate([x0 - x2, x1 - x3], axis=1))
    spectra = jnp.concatenate(
        [
            dot3(split(both + diff), (even_hi[:, :half], even_lo[:, :half])),
            dot3(split(both - diff), (even_hi[:, half:], even_lo[:, half:])),
            dot3(odd, (odd_hi[...], odd_lo[...])),
        ],
        axis=1,
    )

    pl.semaphore_wait(barrier, count - 1)
    for k in range(CHUNKS):
        for side, there, r, target in sides:
            @pl.when(there)
            def _():
                x_copy(0, side, k, r, target).start()
    for r in range(layers):
        send_lat(0, r)
    to_all(lambda q: grav_ref, g_in, g_send, g_recv)
    to_all(lambda q: mat_ref, mat_in, t_send, t_recv)

    parts = []
    for h in range(halves):
        for r in range(layers):
            at = r * rows + 8 * h
            parts.append(
                jnp.concatenate(
                    [
                        spectra[o + at : o + at + 8, t * LANES : (t + 1) * LANES]
                        for t in range(tiles)
                        for o in (0, block)
                    ],
                    axis=0,
                )
            )
    for p, part in enumerate(swap_groups(parts, width)):
        for t in range(tiles):
            pack_out[per_tile * t + p] = part[16 * t : 16 * (t + 1)]
    to_all(lambda q: pack_out.at[q], pack_in, a_send, a_recv)
    pack_in[me] = pack_out[me]

    sub8 = lax.broadcasted_iota(jnp.int32, (8, LANES), 0)
    group8 = lax.broadcasted_iota(jnp.int32, (8, LANES), 1) // width
    for t in range(tiles):
        cols = slice(t * LANES, (t + 1) * LANES)
        x = spectra[2 * block : 2 * block + 8, cols]
        for h in range(1, halves):
            at = 2 * block + 8 * h
            x = jnp.where(rad == h, spectra[at : at + 8, cols], x)
        for step in (1, 2, 4):
            sb, gb = (sub8 // step) % 2, (group8 // step) % 2
            up = pltpu.roll(pltpu.roll(x, 8 - step, 0), width * step, 1)
            down = pltpu.roll(pltpu.roll(x, step, 0), LANES - width * step, 1)
            x = jnp.where(sb == gb, x, jnp.where(gb == 1, up, down))
        for p in range(per_tile):
            ice_out[per_tile * t + p] = x[p : p + 1]
    to_all(lambda q: ice_out.at[q], ice_in, i_send, i_recv)
    ice_in[me] = ice_out[me]

    each(lambda q: grav_ref, g_in, g_send, g_recv, "recv")
    each(lambda q: mat_ref, mat_in, t_send, t_recv, "recv")
    degrees = fwd_hi.shape[0]
    own = degrees // lat_n
    cut = lax.rem(lax.broadcasted_iota(jnp.int32, (own, LANES), 1), own) == (
        lax.broadcasted_iota(jnp.int32, (own, LANES), 0)
    )
    wide = []
    for x in range(rad_n):
        for r in range(layers):
            wide.append(
                jnp.concatenate(
                    [
                        jnp.where(
                            cut, jnp.broadcast_to(g_in[rad_n * i + x, r : r + 1], (own, LANES)), 0.0
                        )
                        for i in range(lat_n)
                    ],
                    axis=0,
                )
            )
    wide = split(jnp.concatenate(wide, axis=1))
    entries = total_rad * total_rad
    gather = jnp.where(
        lax.broadcasted_iota(jnp.int32, (wide[0].shape[1], entries), 0) // own
        == lax.broadcasted_iota(jnp.int32, (wide[0].shape[1], entries), 1),
        1.0, 0.0,
    ).astype(jnp.bfloat16)
    wide = split(
        jnp.dot(wide[0], gather, preferred_element_type=f32)
        + jnp.dot(wide[1], gather, preferred_element_type=f32)
    )
    entry = lax.broadcasted_iota(jnp.int32, (entries, LANES), 0)
    target = lax.broadcasted_iota(jnp.int32, (entries, LANES), 1) // width
    for d in range(total_rad):
        cols = slice(d * LANES, (d + 1) * LANES)
        origin = lax.rem(target + (total_rad - d), total_rad)
        place = jnp.where(entry == target * total_rad + origin, 1.0, 0.0).astype(jnp.bfloat16)
        gexp[:, cols] = jnp.dot(wide[0], place, preferred_element_type=f32) + jnp.dot(
            wide[1], place, preferred_element_type=f32
        )

    jrow = lax.broadcasted_iota(jnp.int32, (rows, LANES), 0)
    jlane = (lax.broadcasted_iota(jnp.int32, (rows, LANES), 1)) % rows
    ids = []
    for i in range(lat_n):
        line = mat_in[rad_n * i]
        for x in range(1, rad_n):
            line = line + mat_in[rad_n * i + x]
        ids.append(jnp.where(jrow == jlane, jnp.broadcast_to(line, (rows, LANES)), 0.0))
    source_layer = lax.broadcasted_iota(jnp.int32, (LANES, LANES), 0)
    source_layer = source_layer // rows
    spread = jnp.where(
        source_layer == lax.broadcasted_iota(jnp.int32, (LANES, LANES), 1) // width, 1.0, 0.0
    ).astype(jnp.bfloat16)
    ids = jnp.dot(
        jnp.concatenate(ids, axis=0).astype(jnp.bfloat16), spread,
        preferred_element_type=f32,
    )
    for n, table in enumerate((mu_ref, dec_ref, con_ref)):
        value = jnp.zeros((total_lat, LANES), f32)
        for k in range(table.shape[0]):
            value = jnp.where(ids == k, table[k], value)
        par[n] = value

    def two(s, carry):
        sweep(s, True)
        return carry

    lax.fori_loop(0, SWEEPS - 1, two, 0)

    each(lambda q: pack_out.at[q], pack_in, a_send, a_recv, "recv")
    each(lambda q: ice_out.at[q], ice_in, i_send, i_recv, "recv")
    near = lax.broadcasted_iota(jnp.int32, (16, LANES), 1) < LANES // 2
    us, qs, ss = [], [], []
    sub = lax.broadcasted_iota(jnp.int32, (8, LANES), 0)
    for i in range(lat_n):
        a, b = pack_in[rad_n * i], pack_in[rad_n * i + 1]
        top = jnp.where(near, a, pltpu.roll(b, LANES // 2, 1))
        low = jnp.where(near, pltpu.roll(a, LANES // 2, 1), b)
        us += [top[:8], low[:8]]
        qs += [top[8:], low[8:]]
        for x in range(rad_n):
            ss.append(
                jnp.where(sub == group8, jnp.broadcast_to(ice_in[rad_n * i + x], (8, LANES)), 0.0)
            )
    u, q, s_hat = (jnp.concatenate(v, axis=0) for v in (us, qs, ss))
    step = width
    while step < LANES:
        s_hat = s_hat + pltpu.roll(s_hat, step, 1)
        step *= 2
    glane = lax.broadcasted_iota(jnp.int32, (total_lat, LANES), 1)
    grow = lax.broadcasted_iota(jnp.int32, (total_lat, LANES), 0)
    s_hat = s_hat * ((glane // width + 1).astype(f32) * (load_scale / total_rad))
    shift = shift_ref[pl.ds(me, 1), :]
    stiff, decay, contrast = par[0], par[1], par[2]
    scaled = weight / stiff
    for n in range(SWEEPS):
        beside = shift * u
        beside += jnp.where(grow == 0, 0.0, pltpu.roll(u, 1, 0))
        beside += jnp.where(grow == total_lat - 1, 0.0, pltpu.roll(u, total_lat - 1, 0))
        beside += jnp.where(glane < width, 0.0, pltpu.roll(u, width, 1))
        beside += jnp.where(glane >= LANES - width, 0.0, pltpu.roll(u, LANES - width, 1))
        update = (s_hat - q) * scaled - relax_factor * u + weight * beside
        u = u + update
        q = decay * q + stiff * update
    rho = contrast * u
    zero = jnp.logical_and(me == 0, lax.rem(glane, width) == 0)
    mean = jnp.sum(jnp.where(zero, rho, 0.0)) / (total_lat * total_rad)
    rho = rho - jnp.where(zero, mean, 0.0)
    coef = dot3((fwd_hi[...], fwd_lo[...]), split(rho))
    phi = gexp[:, :LANES] * coef
    for d in range(1, total_rad):
        phi += gexp[:, d * LANES : (d + 1) * LANES] * pltpu.roll(coef, width * d, 1)
    synth = dot3((inv_hi[...], inv_lo[...]), split(phi))
    near8 = lax.broadcasted_iota(jnp.int32, (8, LANES), 1) < LANES // 2
    for i in range(lat_n):
        a, b = synth[rows * i : rows * i + 8], synth[rows * i + 8 : rows * i + 16]
        back_out[rad_n * i] = jnp.where(near8, a, pltpu.roll(b, LANES // 2, 1))
        back_out[rad_n * i + 1] = jnp.where(near8, pltpu.roll(a, LANES // 2, 1), b)
    to_all(lambda q: back_out.at[q], back_in, b_send, b_recv)
    back_in[me] = back_out[me]

    sweep(SWEEPS - 1, True)

    each(lambda q: back_out.at[q], back_in, b_send, b_recv, "recv")
    parts = swap_groups(
        [
            jnp.concatenate([back_in[per_tile * t + p] for t in range(tiles)], axis=0)
            for p in range(per_tile)
        ],
        width,
    )
    lines = []
    for r in range(layers):
        for h in range(halves):
            part = parts[h * layers + r]
            lines.append(
                jnp.concatenate([part[8 * t : 8 * (t + 1)] for t in range(tiles)], axis=1)
            )
    z = jnp.concatenate(lines, axis=0)
    y0 = dot3(split(z[:, :half]), (even_hi[:, :half], even_lo[:, :half]), True)
    y2 = dot3(split(z[:, half : 2 * half]), (even_hi[:, half:], even_lo[:, half:]), True)
    y13 = dot3(split(z[:, 2 * half :]), (odd_hi[...], odd_lo[...]), True)
    alpha, beta = y13[:, :quarter], y13[:, quarter:]
    plus, minus = y0 + y2, y0 - y2
    for a, value in enumerate((plus + alpha, minus + beta, plus - alpha, minus - beta)):
        cols = slice(a * quarter, (a + 1) * quarter)
        value = value.reshape(layers, rows, quarter)
        p_out[:, :, cols] = value
        sbuf[:, :, cols] += coupling * value

    def rest(s, carry):
        sweep(s, s + 1 < last)
        return carry

    lax.fori_loop(SWEEPS, last, rest, 0)
    u_out[...] = ubuf[last]

    each(lambda q: grav_ref, g_in, g_send, g_recv, "send")
    each(lambda q: mat_ref, mat_in, t_send, t_recv, "send")
    each(lambda q: pack_out.at[q], pack_in, a_send, a_recv, "send")
    each(lambda q: ice_out.at[q], ice_in, i_send, i_recv, "send")
    each(lambda q: back_out.at[q], back_in, b_send, b_recv, "send")

    def drain(s, carry):
        for side, there, r, target in sides:
            @pl.when(there)
            def _():
                for k in range(CHUNKS):
                    x_copy(s, side, k, r, target).wait_send()
        for side, there, _, target in poles:
            @pl.when(there)
            def _():
                for r in range(layers):
                    lat_copy(s, side, r, target).wait_send()
        return carry

    lax.fori_loop(0, last, drain, 0)


def deliver_kernel(*refs):
    count = (len(refs) - 1) // 2
    sem = refs[-1]
    copies = []
    for n in range(count):
        for r in range(refs[n].shape[0]):
            copies.append(
                pltpu.make_async_copy(refs[n].at[r], refs[count + n].at[:, r, :], sem.at[n, r])
            )
    for copy in copies:
        copy.start()
    for copy in copies:
        copy.wait()


def deliver(blocks):
    layers, rows, nlon = blocks[0].shape
    return tuple(
        pl.pallas_call(
            deliver_kernel,
            out_shape=[jax.ShapeDtypeStruct((rows, layers, nlon), jnp.float32)] * len(blocks),
            in_specs=[pl.BlockSpec(memory_space=pltpu.VMEM)] * len(blocks),
            out_specs=[pl.BlockSpec(memory_space=pltpu.HBM)] * len(blocks),
            scratch_shapes=[pltpu.SemaphoreType.DMA((len(blocks), layers))],
            compiler_params=pltpu.CompilerParams(vmem_limit_bytes=4 << 20),
        )(*blocks)
    )


def fused(displacement, memory, ice_class, material, tables, gravity):
    lat_dev, r_dev, nlon = displacement.shape
    lat_n, rad_n = lax.axis_size("lat"), lax.axis_size("rad")
    count, total_lat, total_rad = lat_n * rad_n, lat_n * lat_dev, rad_n * r_dev
    degrees = gravity.shape[0] * lat_n
    width = 2 * MODES // count
    bf16, f32 = jnp.bfloat16, jnp.float32
    even, odd = (split_np(t) for t in radix_tables(nlon, MODES))
    basis, weighted = legendre(total_lat, degrees)
    fwd, inv = split_np(weighted), split_np(basis.T)
    orders = column_orders(MODES).reshape(count, width)
    shift = np.tile(2.0 * np.cos(2.0 * np.pi * orders / nlon), (1, total_rad)).astype(np.float32)
    tabs = [*even, *odd, *fwd, *inv]
    gravity = gravity.transpose(1, 2, 0)
    operands = [
        displacement, memory, ice_class, material.T, gravity, *tables, shift, np.concatenate(tabs, axis=0)
    ]
    operands = [pltpu.with_memory_space_constraint(jnp.asarray(x), pltpu.HBM) for x in operands]
    vmem = pl.BlockSpec(memory_space=pltpu.VMEM)
    hbm = pl.BlockSpec(memory_space=pltpu.HBM)
    dma = pltpu.SemaphoreType.DMA
    steps = 2 * SWEEPS
    block = jax.ShapeDtypeStruct((r_dev, lat_dev, nlon), f32)
    out = pl.pallas_call(
        fused_kernel,
        out_shape=[block] * 3,
        in_specs=[hbm] * len(operands),
        out_specs=[vmem] * 3,
        scratch_shapes=[pltpu.VMEM(x.shape, x.dtype) for x in operands[2:5]]
        + [pltpu.SMEM(x.shape, x.dtype) for x in tables]
        + [
            pltpu.VMEM(shift.shape, f32),
            pltpu.VMEM((1 + r_dev, 8, LANES), f32),
            pltpu.VMEM((r_dev, lat_dev, 1), f32),
            pltpu.VMEM((r_dev, lat_dev, 1), f32),
            pltpu.VMEM((1, LANES), f32),
            pltpu.VMEM((r_dev, LANES), f32),
        ]
        + [pltpu.VMEM(x.shape, x.dtype) for x in tabs]
        + [
            dma((2 * r_dev + 7 + len(tabs),)),
            pltpu.VMEM((steps + 1, r_dev, lat_dev, nlon), f32),
            pltpu.VMEM((r_dev, lat_dev, nlon), f32),
            pltpu.VMEM((steps, 2, lat_dev, nlon), f32),
            pltpu.VMEM((steps, 2, r_dev, 1, nlon), f32),
            pltpu.VMEM((steps, 2, r_dev, 1, nlon), f32),
            pltpu.VMEM((count, r_dev, LANES), f32),
            pltpu.VMEM((count, 1, LANES), f32),
            pltpu.VMEM((count, 16, LANES), f32),
            pltpu.VMEM((count, 16, LANES), f32),
            pltpu.VMEM((count, 1, LANES), f32),
            pltpu.VMEM((count, 1, LANES), f32),
            pltpu.VMEM((count, 8, LANES), f32),
            pltpu.VMEM((count, 8, LANES), f32),
            pltpu.VMEM((degrees, total_rad * LANES), f32),
            pltpu.VMEM((3, total_lat, LANES), f32),
            dma((steps, 2, CHUNKS)), dma((steps, 2, CHUNKS)),
            dma((steps, 2, r_dev)), dma((steps, 2, r_dev)),
        ] + [dma((count,))] * 10,
        compiler_params=pltpu.CompilerParams(
            collective_id=2, has_side_effects=True, vmem_limit_bytes=40 << 20
        ),
    )(*operands)
    return deliver(out)


def fits(lat_dev, r_dev, total_lat, total_rad, rad_n, count, degrees):
    width = 2 * MODES // count
    return (
        rad_n == 2
        and lat_dev == 16
        and width * count == 2 * MODES
        and width * total_rad == LANES
        and rad_n * lat_dev * r_dev == LANES
        and total_rad * (degrees * rad_n // count) == LANES
        and total_rad % 8 == 0
        and r_dev <= 8
        and degrees == 2 * LANES
        and total_lat == 2 * LANES
    )


def per_device(
    displacement, memory, ice_class, material, mu_table, decay_table, contrast_table, gravity_kernel
):
    lat_dev, r_dev, nlon = displacement.shape
    lat_count = lax.axis_size("lat")
    rad_count = lax.axis_size("rad")
    rad_index = lax.axis_index("rad")
    total_lat = lat_count * lat_dev
    total_rad = rad_count * r_dev
    degrees = gravity_kernel.shape[0] * lat_count
    cols = 2 * MODES
    columns = cols // lat_count
    stiff = lookup(material.T, mu_table)[:, :, None]
    decay = lookup(material.T, decay_table)[:, :, None]
    contrast = lookup(material.T, contrast_table)[:, :, None]
    layer_pos = (rad_index * r_dev + jnp.arange(r_dev, dtype=jnp.int32) + 1).astype(
        jnp.float32
    ) / total_rad
    source = load_scale * ice_class.astype(jnp.float32)[None, :, :] * layer_pos[:, None, None]
    devices = lat_count * rad_count
    if fits(lat_dev, r_dev, total_lat, total_rad, rad_count, devices, degrees):
        tables = (mu_table, decay_table, contrast_table)
        return fused(
            displacement, memory, ice_class, material, tables, gravity_kernel
        )
    basis, weighted = legendre(total_lat, degrees)
    projection = jnp.asarray(
        np.concatenate([weighted, np.ones((8, total_lat))]).astype(np.float32)
    )
    weight_sum = jnp.asarray(weighted.sum(axis=1).astype(np.float32))
    basis = jnp.asarray(basis.T.astype(np.float32))
    table = fourier_table(nlon, MODES)
    field, mem, kernel_every = sweeps(
        3,
        displacement.transpose(1, 0, 2),
        memory.transpose(1, 0, 2),
        source,
        stiff,
        decay,
        gravity_kernel.reshape(gravity_kernel.shape[0], -1),
    )
    kernel_every = kernel_every.reshape((degrees,) + gravity_kernel.shape[1:])
    rho = contrast * field
    spectra = jnp.dot(rho.reshape(lat_dev * r_dev, nlon), table, precision=HIGH)
    spread = lax.all_to_all(
        spectra.reshape(r_dev, lat_dev, cols).transpose(1, 0, 2), "lat", split_axis=2, concat_axis=0, tiled=True
    )
    coef_cols = jnp.dot(
        projection, spread.reshape(total_lat, r_dev * columns), precision=HIGH
    ).reshape(degrees + 8, r_dev, columns)
    coef_all = lax.all_gather(coef_cols, "rad", axis=1, tiled=True)
    first_order = (lax.axis_index("lat") * columns + jnp.arange(columns, dtype=jnp.int32)) == 0
    mean_row = jnp.sum(coef_all[degrees], axis=0) / (total_lat * total_rad)
    mean_row = jnp.where(first_order, mean_row, 0.0)
    coef_all = coef_all[:degrees] - weight_sum[:, None, None] * mean_row[None, None, :]
    phi_cols = jnp.sum(kernel_every[:, :, :, None] * coef_all[:, None, :, :], axis=2)
    synth_cols = jnp.dot(
        basis, phi_cols.reshape(degrees, r_dev * columns), precision=HIGH
    ).reshape(total_lat, r_dev, columns)
    synth = lax.all_to_all(synth_cols, "lat", split_axis=0, concat_axis=2, tiled=True)
    potential = lax.dot_general(
        synth.transpose(1, 0, 2).reshape(r_dev * lat_dev, cols), table, (((1,), (1,)), ((), ())), precision=HIGH
    ).reshape(r_dev, lat_dev, nlon)
    loaded = source + coupling * potential
    field, mem = sweeps(3, field, mem, loaded, stiff, decay)
    return tuple(x.transpose(1, 0, 2) for x in (field, mem, potential))


def solution(mesh):
    placed = (
        P("lat", "rad", None),
        P("lat", "rad", None),
        P("lat", None),
        P("lat", "rad"),
        P(),
        P(),
        P(),
        P("lat", "rad", None),
    )
    return jax.shard_map(
        per_device,
        mesh=mesh,
        in_specs=placed,
        out_specs=(P("lat", "rad", None), P("lat", "rad", None), P("lat", "rad", None)),
        check_vma=False,
    )
```

```python
import jax
import jax.numpy as jnp
import numpy as np
from jax import lax
from jax.experimental import pallas as pl
from jax.experimental.pallas import tpu as pltpu
from jax.sharding import PartitionSpec as P

MODES = 256


load_scale = 0.5
kappa_shift = 0.5
relax_factor = 0.8
coupling = 2.0
HIGH = lax.Precision.HIGH


def lookup(material, table):
    onehot = (
        material[:, :, None] == jnp.arange(table.shape[0], dtype=jnp.int32)[None, None, :]
    ).astype(jnp.float32)
    return jnp.sum(onehot * table[None, None, :], axis=-1)


def fourier_parts(nlon, modes, minor=128):
    order = np.arange(modes)
    parts = []
    for place in (np.arange(nlon // minor) * minor, np.arange(minor)):
        angle = (place[:, None] * order[None, :] % nlon) * (2.0 * np.pi / nlon)
        parts += [np.cos(angle), np.sin(angle)]
    scale = np.sqrt(2.0 / nlon)
    return [(part * f).astype(np.float32) for part, f in zip(parts, (scale, scale, 1.0, 1.0))]


def fourier_table(nlon, modes):
    ca, sa, cb, sb = lax.optimization_barrier([jnp.asarray(p) for p in fourier_parts(nlon, modes)])
    ca, sa, cb, sb = ca[:, None], sa[:, None], cb[None], sb[None]
    cos = (ca * cb - sa * sb).reshape(nlon, modes)
    sin = (sa * cb + ca * sb).reshape(nlon, modes)
    return jnp.concatenate([cos, sin], axis=1)


def legendre(lat, degrees):
    theta = np.pi * (np.arange(lat) + 0.5) / lat
    cosine = np.cos(theta)
    before, current, rows = np.zeros(lat), np.ones(lat), []
    for n in range(degrees):
        rows.append(current * np.sqrt(n + 0.5))
        before, current = current, ((2.0 * n + 1.0) * cosine * current - n * before) / (n + 1.0)
    basis = np.stack(rows)
    weighted = basis * (np.pi / lat * np.sin(theta))[None, :]
    return basis, weighted


def sweeps_kernel(steps, gather, *refs):
    if gather:
        f_ref, m_ref, s_ref, stiff_ref, decay_ref, g_ref, f_out, m_out, g_out, *refs = refs
        f_buf, face, lat_in, rad_in, send, recv, g_in, g_send, g_recv = refs
    else:
        f_ref, m_ref, s_ref, stiff_ref, decay_ref, f_out, m_out, *refs = refs
        f_buf, face, lat_in, rad_in, send, recv = refs
    layers, rows, nlon = f_ref.shape
    lat_n, rad_n = lax.axis_size("lat"), lax.axis_size("rad")
    lat, rad = lax.axis_index("lat"), lax.axis_index("rad")
    north = (lax.rem(lat + lat_n - 1, lat_n), rad)
    south = (lax.rem(lat + 1, lat_n), rad)
    below = (lat, lax.rem(rad + rad_n - 1, rad_n))
    above = (lat, lax.rem(rad + 1, rad_n))
    if gather:
        peers = [(lax.rem(lat + d, lat_n), rad) for d in range(1, lat_n)] + [below, above]
    else:
        peers = [north, south, below, above]
    barrier = pltpu.get_barrier_semaphore()
    for peer in peers:
        pl.semaphore_signal(barrier, inc=1, device_id=peer, device_id_type=pl.DeviceIdType.MESH)
    pl.semaphore_wait(barrier, len(peers))

    def remote(src, dst, send_sem, recv_sem, peer):
        copy = pltpu.make_async_remote_copy(
            src_ref=src, dst_ref=dst, send_sem=send_sem, recv_sem=recv_sem,
            device_id=peer, device_id_type=pl.DeviceIdType.MESH,
        )
        copy.start()
        return copy

    weight = relax_factor / (6.0 + kappa_shift)
    w_north = jnp.where(lat > 0, weight, 0.0)
    w_south = jnp.where(lat < lat_n - 1, weight, 0.0)
    w_below = jnp.where(rad > 0, weight, 0.0)
    w_above = jnp.where(rad < rad_n - 1, weight, 0.0)
    row = lax.broadcasted_iota(jnp.int32, (rows, nlon), 0)
    gathered = []
    for step in range(steps):
        old = f_ref if step == 0 else f_buf.at[step - 1]
        new = f_out if step == steps - 1 else f_buf.at[step]
        old_m = m_ref if step == 0 else m_out
        for r in range(layers):
            face[step, 0, r : r + 1, :] = old[r, 0:1, :]
            face[step, 1, r : r + 1, :] = old[r, rows - 1 : rows, :]
        copies = [
            remote(old.at[0], rad_in.at[step, 1], send.at[step, 0], recv.at[step, 0], below),
            remote(old.at[layers - 1], rad_in.at[step, 0], send.at[step, 1], recv.at[step, 1], above),
            remote(face.at[step, 0], lat_in.at[step, 1], send.at[step, 2], recv.at[step, 2], north),
            remote(face.at[step, 1], lat_in.at[step, 0], send.at[step, 3], recv.at[step, 3], south),
        ]
        if gather and step == 0:
            gathered = [
                remote(g_ref, g_in.at[lat], g_send.at[d], g_recv.at[d], peers[d - 1])
                for d in range(1, lat_n)
            ]
        for r in range(layers):
            f, m = old[r], old_m[r]
            beside = pltpu.roll(f, 1, 1) + pltpu.roll(f, nlon - 1, 1)
            beside += jnp.where(row == 0, 0.0, pltpu.roll(f, 1, 0))
            beside += jnp.where(row == rows - 1, 0.0, pltpu.roll(f, rows - 1, 0))
            if r > 0:
                beside += old[r - 1]
            if r < layers - 1:
                beside += old[r + 1]
            stiff = stiff_ref[r]
            update = (s_ref[r] - m) * (weight / stiff) - relax_factor * f + weight * beside
            new[r] = f + update
            m_out[r] = decay_ref[r] * m + stiff * update
        for copy in copies:
            copy.wait()
        for r, slot, w in ((0, 0, w_below), (layers - 1, 1, w_above)):
            extra = w * rad_in[step, slot]
            new[r] += extra
            m_out[r] += stiff_ref[r] * extra
        for r in range(layers):
            for j, slot, w in ((0, 0, w_north), (rows - 1, 1, w_south)):
                extra = w * lat_in[step, slot, r : r + 1, :]
                new[r, j : j + 1, :] += extra
                m_out[r, j : j + 1, :] += stiff_ref[r, j : j + 1, :] * extra
    if gather:
        for copy in gathered:
            copy.wait()
        g_in[lat] = g_ref[...]
        g_out[...] = g_in[...]


def sweeps(steps, field, memory, source, stiff, decay, gravity=None):
    gather = gravity is not None
    layers, rows, nlon = field.shape
    block = jax.ShapeDtypeStruct(field.shape, jnp.float32)
    operands, out = [field, memory, source, stiff, decay], [block, block]
    dma, f32 = pltpu.SemaphoreType.DMA, jnp.float32
    scratch = [
        pltpu.VMEM((steps - 1, layers, rows, nlon), f32),
        pltpu.VMEM((steps, 2, layers, nlon), f32),
        pltpu.VMEM((steps, 2, layers, nlon), f32),
        pltpu.VMEM((steps, 2, rows, nlon), f32),
        dma((steps, 4)),
        dma((steps, 4)),
    ]
    if gather:
        lat_n = lax.axis_size("lat")
        every = (lat_n,) + gravity.shape
        operands.append(gravity)
        out.append(jax.ShapeDtypeStruct(every, f32))
        scratch += [pltpu.VMEM(every, f32), dma((lat_n,)), dma((lat_n,))]
    vmem = pl.BlockSpec(memory_space=pltpu.VMEM)

    def kernel(*refs):
        sweeps_kernel(steps, gather, *refs)

    return pl.pallas_call(
        kernel,
        out_shape=out,
        in_specs=[vmem] * len(operands),
        out_specs=[vmem] * len(out),
        scratch_shapes=scratch,
        compiler_params=pltpu.CompilerParams(
            collective_id=0 if gather else 1, has_side_effects=True
        ),
    )(*operands)


LANES = 128
CHUNKS = 4
SWEEPS = 3


def split_np(x):
    x = np.asarray(x, np.float32)
    hi = x.astype(jnp.bfloat16)
    return hi, (x - hi.astype(np.float32)).astype(jnp.bfloat16)


def split(x):
    hi = x.astype(jnp.bfloat16)
    return hi, (x - hi.astype(jnp.float32)).astype(jnp.bfloat16)


def dot3(left, right, transposed=False):
    dims = (((1,), (1 if transposed else 0,)), ((), ()))

    def one(a, b):
        return lax.dot_general(a, b, dims, preferred_element_type=jnp.float32)

    return one(left[0], right[0]) + (one(left[0], right[1]) + one(left[1], right[0]))


def radix_tables(nlon, modes):
    quarter, per = nlon // 4, modes // 4
    place = np.arange(quarter)[:, None]

    def waves(k):
        order = k + 4 * np.arange(per)[None, :]
        angle = (place * order % nlon) * (2.0 * np.pi / nlon)
        return np.sqrt(2.0 / nlon) * np.cos(angle), np.sqrt(2.0 / nlon) * np.sin(angle)

    (c0, s0), (c1, s1), (c2, s2), (c3, s3) = (waves(k) for k in range(4))
    even = np.concatenate([c0, s0, c2, s2], axis=1)
    odd = np.concatenate(
        [np.concatenate([c1, s1, c3, s3], axis=1), np.concatenate([-s1, c1, s3, -c3], axis=1)],
        axis=0,
    )
    return even, odd


def column_orders(modes):
    per = np.arange(modes // 4)
    return np.concatenate([k + 4 * per for k in (0, 0, 2, 2, 1, 1, 3, 3)])


def swap_groups(parts, width):
    parts, step = list(parts), 1
    lane = lax.broadcasted_iota(jnp.int32, parts[0].shape, 1)
    while step < len(parts):
        low = (lane // (width * step)) % 2 == 0
        for g in range(len(parts)):
            if (g // step) % 2 == 0:
                a, b = parts[g], parts[g + step]
                parts[g] = jnp.where(low, a, pltpu.roll(b, width * step, 1))
                parts[g + step] = jnp.where(low, pltpu.roll(a, LANES - width * step, 1), b)
        step *= 2
    return parts


def fused_kernel(
    u_ref, m_ref, ice_hbm, material_hbm, gravity_hbm, mu_hbm, dec_hbm, con_hbm, shift_hbm, table_hbm,
    u_out, m_out, p_out,
    ice_ref, material, gravity, mu_ref, dec_ref, con_ref, shift_ref, pad,
    stiff_ref, decay_ref, grav_ref,
    even_hi, even_lo, odd_hi, odd_lo, fwd_hi, fwd_lo, inv_hi, inv_lo, load_sem,
    ubuf, sbuf, x_in, lat_out, lat_in, g_in, pack_out, pack_in,
    back_out, back_in, gexp, par,
    x_send, x_recv, l_send, l_recv, g_send, g_recv, a_send, a_recv, b_send, b_recv,
):
    f32 = jnp.float32
    rows, layers, nlon = u_ref.shape
    lat_n, rad_n = lax.axis_size("lat"), lax.axis_size("rad")
    lat, rad = lax.axis_index("lat"), lax.axis_index("rad")
    count = lat_n * rad_n
    me = lat * rad_n + rad
    total_lat, total_rad = lat_n * rows, rad_n * layers
    halves = rows // 8
    width = LANES // (halves * layers)
    tiles = count * width // LANES
    per_tile = LANES // width
    chunk = nlon // CHUNKS
    last = 2 * SWEEPS
    weight = relax_factor / (6.0 + kappa_shift)

    def device(index):
        return (index // rad_n, lax.rem(index, rad_n))

    def peer(d):
        return lax.rem(me + d, count)

    barrier = pltpu.get_barrier_semaphore()

    def greet(d, carry):
        pl.semaphore_signal(
            barrier, inc=1, device_id=device(peer(d)), device_id_type=pl.DeviceIdType.MESH
        )
        return carry

    lax.fori_loop(1, count, greet, 0)

    pairs = [(u_ref.at[:, r, :], ubuf.at[0, r]) for r in range(layers)]
    pairs += [(m_ref.at[:, r, :], m_out.at[r]) for r in range(layers)]
    pairs += [
        (ice_hbm, ice_ref), (material_hbm, material), (gravity_hbm, gravity), (mu_hbm, mu_ref),
        (dec_hbm, dec_ref), (con_hbm, con_ref), (shift_hbm, shift_ref),
    ]
    first = len(pairs)
    at = 0
    for held in (even_hi, even_lo, odd_hi, odd_lo, fwd_hi, fwd_lo, inv_hi, inv_lo):
        pairs.append((table_hbm.at[pl.ds(at, held.shape[0])], held))
        at += held.shape[0]
    loads = [pltpu.make_async_copy(a, b, load_sem.at[n]) for n, (a, b) in enumerate(pairs)]
    for load in loads:
        load.start()

    def remote(src, dst, send_sem, recv_sem, target):
        return pltpu.make_async_remote_copy(
            src_ref=src, dst_ref=dst, send_sem=send_sem, recv_sem=recv_sem,
            device_id=target, device_id_type=pl.DeviceIdType.MESH,
        )

    def to_all(src_of, dst, send_sem, recv_sem):
        def start(d, carry):
            far = d // 2
            d = count // 2 + jnp.where(lax.rem(d, 2) == 1, far, -far)
            q = peer(d)
            remote(src_of(q), dst.at[me], send_sem.at[d], recv_sem.at[d], device(q)).start()
            return carry

        lax.fori_loop(1, count, start, 0)

    def each(src_of, dst, send_sem, recv_sem, how):
        def wait(d, carry):
            q = peer(d)
            copy = remote(src_of(q), dst.at[me], send_sem.at[d], recv_sem.at[d], device(q))
            copy.wait_recv() if how == "recv" else copy.wait_send()
            return carry

        lax.fori_loop(1, count, wait, 0)

    sides = (
        (0, rad > 0, 0, (lat, jnp.maximum(rad - 1, 0))),
        (1, rad < rad_n - 1, layers - 1, (lat, jnp.minimum(rad + 1, rad_n - 1))),
    )

    def x_copy(s, side, k, r, target):
        cols = pl.ds(k * chunk, chunk)
        return remote(
            ubuf.at[s, r, :, cols], x_in.at[s, 1 - side, :, cols],
            x_send.at[s, side, k], x_recv.at[s, 1 - side, k], target,
        )

    poles = (
        (0, lat > 0, 0, (jnp.maximum(lat - 1, 0), rad)),
        (1, lat < lat_n - 1, rows - 1, (jnp.minimum(lat + 1, lat_n - 1), rad)),
    )

    def lat_copy(s, side, r, target):
        return remote(
            lat_out.at[s, side, r], lat_in.at[s, 1 - side, r],
            l_send.at[s, side, r], l_recv.at[s, 1 - side, r], target,
        )

    def send_lat(s, r):
        for side, there, j, target in poles:
            @pl.when(there)
            def _():
                lat_out[s, side, r] = ubuf[s, r, j : j + 1, :]
                lat_copy(s, side, r, target).start()

    def sweep(s, more):
        row = lax.broadcasted_iota(jnp.int32, (rows, nlon), 0)

        def forward(r, when):
            @pl.when(jnp.logical_and(when, more))
            def _():
                send_lat(s + 1, r)

        def inner(r):
            for side, there, _, target in poles:
                @pl.when(there)
                def _():
                    lat_copy(s, 1 - side, r, target).wait_recv()

            f, m = ubuf[s, r], m_out[r]
            beside = pltpu.roll(f, 1, 1) + pltpu.roll(f, nlon - 1, 1)
            beside += jnp.where(row == 0, lat_in[s, 0, r], pltpu.roll(f, 1, 0))
            beside += jnp.where(row == rows - 1, lat_in[s, 1, r], pltpu.roll(f, rows - 1, 0))
            if r > 0:
                beside += ubuf[s, r - 1]
            if r < layers - 1:
                beside += ubuf[s, r + 1]
            stiff = stiff_ref[r]
            update = (sbuf[r] - m) * (weight / stiff) - relax_factor * f + weight * beside
            ubuf[s + 1, r] = f + update
            m_out[r] = decay_ref[r] * m + stiff * update
            alone = True
            for side, there, edge, _ in sides:
                if edge == r:
                    alone = jnp.logical_not(there)
            forward(r, alone)

        rest = list(range(1, layers - 1))
        inner(layers - 1)
        inner(0)
        for k in range(CHUNKS):
            for side, there, r, target in sides:
                @pl.when(there)
                def _():
                    cols = slice(k * chunk, (k + 1) * chunk)
                    x_copy(s, 1 - side, k, r, target).wait_recv()
                    extra = weight * x_in[s, side, :, cols]
                    ubuf[s + 1, r, :, cols] += extra
                    m_out[r, :, cols] += stiff_ref[r] * extra
                    if more is True:
                        x_copy(s + 1, side, k, r, target).start()
                    else:
                        @pl.when(more)
                        def _():
                            x_copy(s + 1, side, k, r, target).start()
            if k < len(rest):
                inner(rest[k])

        for side, there, r, _ in sides:
            forward(r, there)

    for side, there, _, _ in poles:
        @pl.when(jnp.logical_not(there))
        def _():
            for s in range(last):
                lat_in[s, side] = jnp.zeros(lat_in.shape[2:], f32)
    for load in loads[:first]:
        load.wait()
    pad[...] = jnp.zeros_like(pad)
    pad[0, :layers, :rows] = material[...].astype(f32)
    own = gravity.shape[2]
    for r in range(layers):
        pad[1 + r, :, :own] = gravity[r]
    prow = lax.broadcasted_iota(jnp.int32, (rows, LANES), 0)
    plane = lax.broadcasted_iota(jnp.int32, (rows, LANES), 1)
    line = jnp.zeros((1, LANES), f32)
    for r in range(layers):
        kind = pad[0, r : r + 1]
        for x in range(rad_n):
            at = (x * layers + r) * rows
            line += jnp.where(rad == x, pltpu.roll(kind, at, 1) if at else kind, 0.0)
        column = jnp.sum(jnp.where(prow == plane, kind, 0.0), axis=1, keepdims=True)
        for table, held in ((mu_ref, stiff_ref), (dec_ref, decay_ref)):
            value = jnp.zeros((rows, 1), f32)
            for k in range(table.shape[0]):
                value = jnp.where(column == k, table[k], value)
            held[r] = value
        full = pad[1 + r]
        step = own
        while step < LANES:
            full = full + pltpu.roll(full, step, 1)
            step *= 2
        keep = lax.broadcasted_iota(jnp.int32, full.shape, 1) // own == lax.broadcasted_iota(
            jnp.int32, full.shape, 0
        )
        grav_ref[r : r + 1] = jnp.sum(jnp.where(keep, full, 0.0), axis=0, keepdims=True)
    grav_ref[layers : layers + 1] = line
    g_in[me] = grav_ref[...]
    ice = ice_ref[...].astype(f32)
    for r in range(layers):
        pos = (rad * layers + (r + 1)).astype(f32) / total_rad
        sbuf[r] = (load_scale * pos) * ice
    for load in loads[first:]:
        load.wait()

    quarter = nlon // 4
    block = layers * rows

    def piece(a):
        cols = slice(a * quarter, (a + 1) * quarter)
        return jnp.concatenate(
            [
                ubuf[0, :, :, cols].reshape(block, quarter),
                m_out[:, :, cols].reshape(block, quarter),
                ice_ref[:, cols].astype(f32),
            ],
            axis=0,
        )

    x0, x1, x2, x3 = (piece(a) for a in range(4))
    half = even_hi.shape[1] // 2
    both, diff = x0 + x2, x1 + x3
    odd = split(jnp.concatenate([x0 - x2, x1 - x3], axis=1))
    spectra = jnp.concatenate(
        [
            dot3(split(both + diff), (even_hi[:, :half], even_lo[:, :half])),
            dot3(split(both - diff), (even_hi[:, half:], even_lo[:, half:])),
            dot3(odd, (odd_hi[...], odd_lo[...])),
        ],
        axis=1,
    )

    pl.semaphore_wait(barrier, count - 1)
    for k in range(CHUNKS):
        for side, there, r, target in sides:
            @pl.when(there)
            def _():
                x_copy(0, side, k, r, target).start()
    for r in range(layers):
        send_lat(0, r)
    to_all(lambda q: grav_ref, g_in, g_send, g_recv)

    parts = []
    for h in range(halves):
        for r in range(layers):
            at = r * rows + 8 * h
            parts.append(
                jnp.concatenate(
                    [
                        spectra[o + at : o + at + 8, t * LANES : (t + 1) * LANES]
                        for t in range(tiles)
                        for o in (0, block)
                    ],
                    axis=0,
                )
            )
    for p, part in enumerate(swap_groups(parts, width)):
        for t in range(tiles):
            pack_out[per_tile * t + p, 0:16] = part[16 * t : 16 * (t + 1)]

    sub8 = lax.broadcasted_iota(jnp.int32, (8, LANES), 0)
    group8 = lax.broadcasted_iota(jnp.int32, (8, LANES), 1) // width
    for t in range(tiles):
        cols = slice(t * LANES, (t + 1) * LANES)
        x = spectra[2 * block : 2 * block + 8, cols]
        for h in range(1, halves):
            at = 2 * block + 8 * h
            x = jnp.where(rad == h, spectra[at : at + 8, cols], x)
        for step in (1, 2, 4):
            sb, gb = (sub8 // step) % 2, (group8 // step) % 2
            up = pltpu.roll(pltpu.roll(x, 8 - step, 0), width * step, 1)
            down = pltpu.roll(pltpu.roll(x, step, 0), LANES - width * step, 1)
            x = jnp.where(sb == gb, x, jnp.where(gb == 1, up, down))
        for p in range(per_tile):
            pack_out[per_tile * t + p, 16:17] = x[p : p + 1]
    to_all(lambda q: pack_out.at[q], pack_in, a_send, a_recv)
    pack_in[me] = pack_out[me]

    each(lambda q: grav_ref, g_in, g_send, g_recv, "recv")
    degrees = fwd_hi.shape[0]
    own = degrees // lat_n
    cut = lax.rem(lax.broadcasted_iota(jnp.int32, (own, LANES), 1), own) == (
        lax.broadcasted_iota(jnp.int32, (own, LANES), 0)
    )
    wide = []
    for x in range(rad_n):
        for r in range(layers):
            wide.append(
                jnp.concatenate(
                    [
                        jnp.where(
                            cut, jnp.broadcast_to(g_in[rad_n * i + x, r : r + 1], (own, LANES)), 0.0
                        )
                        for i in range(lat_n)
                    ],
                    axis=0,
                )
            )
    wide = split(jnp.concatenate(wide, axis=1))
    entries = total_rad * total_rad
    gather = jnp.where(
        lax.broadcasted_iota(jnp.int32, (wide[0].shape[1], entries), 0) // own
        == lax.broadcasted_iota(jnp.int32, (wide[0].shape[1], entries), 1),
        1.0, 0.0,
    ).astype(jnp.bfloat16)
    wide = split(
        jnp.dot(wide[0], gather, preferred_element_type=f32)
        + jnp.dot(wide[1], gather, preferred_element_type=f32)
    )
    entry = lax.broadcasted_iota(jnp.int32, (entries, LANES), 0)
    target = lax.broadcasted_iota(jnp.int32, (entries, LANES), 1) // width
    for d in range(total_rad):
        cols = slice(d * LANES, (d + 1) * LANES)
        origin = lax.rem(target + (total_rad - d), total_rad)
        place = jnp.where(entry == target * total_rad + origin, 1.0, 0.0).astype(jnp.bfloat16)
        gexp[:, cols] = jnp.dot(wide[0], place, preferred_element_type=f32) + jnp.dot(
            wide[1], place, preferred_element_type=f32
        )

    jrow = lax.broadcasted_iota(jnp.int32, (rows, LANES), 0)
    jlane = (lax.broadcasted_iota(jnp.int32, (rows, LANES), 1)) % rows
    ids = []
    for i in range(lat_n):
        line = g_in[rad_n * i, layers : layers + 1]
        for x in range(1, rad_n):
            line = line + g_in[rad_n * i + x, layers : layers + 1]
        ids.append(jnp.where(jrow == jlane, jnp.broadcast_to(line, (rows, LANES)), 0.0))
    source_layer = lax.broadcasted_iota(jnp.int32, (LANES, LANES), 0)
    source_layer = source_layer // rows
    spread = jnp.where(
        source_layer == lax.broadcasted_iota(jnp.int32, (LANES, LANES), 1) // width, 1.0, 0.0
    ).astype(jnp.bfloat16)
    ids = jnp.dot(
        jnp.concatenate(ids, axis=0).astype(jnp.bfloat16), spread,
        preferred_element_type=f32,
    )
    for n, table in enumerate((mu_ref, dec_ref, con_ref)):
        value = jnp.zeros((total_lat, LANES), f32)
        for k in range(table.shape[0]):
            value = jnp.where(ids == k, table[k], value)
        par[n] = value

    def two(s, carry):
        sweep(s, True)
        return carry

    lax.fori_loop(0, 1, two, 0)

    each(lambda q: pack_out.at[q], pack_in, a_send, a_recv, "recv")
    near = lax.broadcasted_iota(jnp.int32, (16, LANES), 1) < LANES // 2
    us, qs, ss = [], [], []
    sub = lax.broadcasted_iota(jnp.int32, (8, LANES), 0)
    for i in range(lat_n):
        a, b = pack_in[rad_n * i, 0:16], pack_in[rad_n * i + 1, 0:16]
        top = jnp.where(near, a, pltpu.roll(b, LANES // 2, 1))
        low = jnp.where(near, pltpu.roll(a, LANES // 2, 1), b)
        us += [top[:8], low[:8]]
        qs += [top[8:], low[8:]]
        for x in range(rad_n):
            ss.append(
                jnp.where(
                    sub == group8,
                    jnp.broadcast_to(pack_in[rad_n * i + x, 16:17], (8, LANES)),
                    0.0,
                )
            )
    u, q, s_hat = (jnp.concatenate(v, axis=0) for v in (us, qs, ss))
    step = width
    while step < LANES:
        s_hat = s_hat + pltpu.roll(s_hat, step, 1)
        step *= 2
    glane = lax.broadcasted_iota(jnp.int32, (total_lat, LANES), 1)
    grow = lax.broadcasted_iota(jnp.int32, (total_lat, LANES), 0)
    s_hat = s_hat * ((glane // width + 1).astype(f32) * (load_scale / total_rad))
    shift = shift_ref[pl.ds(me, 1), :]
    stiff, decay, contrast = par[0], par[1], par[2]
    scaled = weight / stiff
    for n in range(SWEEPS):
        beside = shift * u
        beside += jnp.where(grow == 0, 0.0, pltpu.roll(u, 1, 0))
        beside += jnp.where(grow == total_lat - 1, 0.0, pltpu.roll(u, total_lat - 1, 0))
        beside += jnp.where(glane < width, 0.0, pltpu.roll(u, width, 1))
        beside += jnp.where(glane >= LANES - width, 0.0, pltpu.roll(u, LANES - width, 1))
        update = (s_hat - q) * scaled - relax_factor * u + weight * beside
        u = u + update
        q = decay * q + stiff * update
    rho = contrast * u
    zero = jnp.logical_and(me == 0, lax.rem(glane, width) == 0)
    mean = jnp.sum(jnp.where(zero, rho, 0.0)) / (total_lat * total_rad)
    rho = rho - jnp.where(zero, mean, 0.0)
    coef = dot3((fwd_hi[...], fwd_lo[...]), split(rho))
    phi = gexp[:, :LANES] * coef
    for d in range(1, total_rad):
        phi += gexp[:, d * LANES : (d + 1) * LANES] * pltpu.roll(coef, width * d, 1)
    synth = dot3((inv_hi[...], inv_lo[...]), split(phi))
    near8 = lax.broadcasted_iota(jnp.int32, (8, LANES), 1) < LANES // 2
    for i in range(lat_n):
        a, b = synth[rows * i : rows * i + 8], synth[rows * i + 8 : rows * i + 16]
        back_out[rad_n * i] = jnp.where(near8, a, pltpu.roll(b, LANES // 2, 1))
        back_out[rad_n * i + 1] = jnp.where(near8, pltpu.roll(a, LANES // 2, 1), b)
    to_all(lambda q: back_out.at[q], back_in, b_send, b_recv)
    back_in[me] = back_out[me]

    lax.fori_loop(1, SWEEPS, two, 0)

    each(lambda q: back_out.at[q], back_in, b_send, b_recv, "recv")
    parts = swap_groups(
        [
            jnp.concatenate([back_in[per_tile * t + p] for t in range(tiles)], axis=0)
            for p in range(per_tile)
        ],
        width,
    )
    lines = []
    for r in range(layers):
        for h in range(halves):
            part = parts[h * layers + r]
            lines.append(
                jnp.concatenate([part[8 * t : 8 * (t + 1)] for t in range(tiles)], axis=1)
            )
    z = jnp.concatenate(lines, axis=0)
    y0 = dot3(split(z[:, :half]), (even_hi[:, :half], even_lo[:, :half]), True)
    y2 = dot3(split(z[:, half : 2 * half]), (even_hi[:, half:], even_lo[:, half:]), True)
    y13 = dot3(split(z[:, 2 * half :]), (odd_hi[...], odd_lo[...]), True)
    alpha, beta = y13[:, :quarter], y13[:, quarter:]
    plus, minus = y0 + y2, y0 - y2
    for a, value in enumerate((plus + alpha, minus + beta, plus - alpha, minus - beta)):
        cols = slice(a * quarter, (a + 1) * quarter)
        value = value.reshape(layers, rows, quarter)
        p_out[:, :, cols] = value
        sbuf[:, :, cols] += coupling * value

    def rest(s, carry):
        sweep(s, s + 1 < last)
        return carry

    lax.fori_loop(SWEEPS, last, rest, 0)
    u_out[...] = ubuf[last]

    each(lambda q: grav_ref, g_in, g_send, g_recv, "send")
    each(lambda q: pack_out.at[q], pack_in, a_send, a_recv, "send")
    each(lambda q: back_out.at[q], back_in, b_send, b_recv, "send")

    def drain(s, carry):
        for side, there, r, target in sides:
            @pl.when(there)
            def _():
                for k in range(CHUNKS):
                    x_copy(s, side, k, r, target).wait_send()
        for side, there, _, target in poles:
            @pl.when(there)
            def _():
                for r in range(layers):
                    lat_copy(s, side, r, target).wait_send()
        return carry

    lax.fori_loop(0, last, drain, 0)


def deliver_kernel(*refs):
    count = (len(refs) - 1) // 2
    sem = refs[-1]
    copies = []
    for n in range(count):
        for r in range(refs[n].shape[0]):
            copies.append(
                pltpu.make_async_copy(refs[n].at[r], refs[count + n].at[:, r, :], sem.at[n, r])
            )
    for copy in copies:
        copy.start()
    for copy in copies:
        copy.wait()


def deliver(blocks):
    layers, rows, nlon = blocks[0].shape
    return tuple(
        pl.pallas_call(
            deliver_kernel,
            out_shape=[jax.ShapeDtypeStruct((rows, layers, nlon), jnp.float32)] * len(blocks),
            in_specs=[pl.BlockSpec(memory_space=pltpu.VMEM)] * len(blocks),
            out_specs=[pl.BlockSpec(memory_space=pltpu.HBM)] * len(blocks),
            scratch_shapes=[pltpu.SemaphoreType.DMA((len(blocks), layers))],
            compiler_params=pltpu.CompilerParams(vmem_limit_bytes=4 << 20),
        )(*blocks)
    )


def fused(displacement, memory, ice_class, material, tables, gravity):
    lat_dev, r_dev, nlon = displacement.shape
    lat_n, rad_n = lax.axis_size("lat"), lax.axis_size("rad")
    count, total_lat, total_rad = lat_n * rad_n, lat_n * lat_dev, rad_n * r_dev
    degrees = gravity.shape[0] * lat_n
    width = 2 * MODES // count
    bf16, f32 = jnp.bfloat16, jnp.float32
    even, odd = (split_np(t) for t in radix_tables(nlon, MODES))
    basis, weighted = legendre(total_lat, degrees)
    fwd, inv = split_np(weighted), split_np(basis.T)
    orders = column_orders(MODES).reshape(count, width)
    shift = np.tile(2.0 * np.cos(2.0 * np.pi * orders / nlon), (1, total_rad)).astype(np.float32)
    tabs = [*even, *odd, *fwd, *inv]
    gravity = gravity.transpose(1, 2, 0)
    operands = [
        displacement, memory, ice_class, material.T, gravity, *tables, shift, np.concatenate(tabs, axis=0)
    ]
    operands = [pltpu.with_memory_space_constraint(jnp.asarray(x), pltpu.HBM) for x in operands]
    vmem = pl.BlockSpec(memory_space=pltpu.VMEM)
    hbm = pl.BlockSpec(memory_space=pltpu.HBM)
    dma = pltpu.SemaphoreType.DMA
    steps = 2 * SWEEPS
    block = jax.ShapeDtypeStruct((r_dev, lat_dev, nlon), f32)
    out = pl.pallas_call(
        fused_kernel,
        out_shape=[block] * 3,
        in_specs=[hbm] * len(operands),
        out_specs=[vmem] * 3,
        scratch_shapes=[pltpu.VMEM(x.shape, x.dtype) for x in operands[2:5]]
        + [pltpu.SMEM(x.shape, x.dtype) for x in tables]
        + [
            pltpu.VMEM(shift.shape, f32),
            pltpu.VMEM((1 + r_dev, 8, LANES), f32),
            pltpu.VMEM((r_dev, lat_dev, 1), f32),
            pltpu.VMEM((r_dev, lat_dev, 1), f32),
            pltpu.VMEM((r_dev + 1, LANES), f32),
        ]
        + [pltpu.VMEM(x.shape, x.dtype) for x in tabs]
        + [
            dma((2 * r_dev + 7 + len(tabs),)),
            pltpu.VMEM((steps + 1, r_dev, lat_dev, nlon), f32),
            pltpu.VMEM((r_dev, lat_dev, nlon), f32),
            pltpu.VMEM((steps, 2, lat_dev, nlon), f32),
            pltpu.VMEM((steps, 2, r_dev, 1, nlon), f32),
            pltpu.VMEM((steps, 2, r_dev, 1, nlon), f32),
            pltpu.VMEM((count, r_dev + 1, LANES), f32),
            pltpu.VMEM((count, 17, LANES), f32),
            pltpu.VMEM((count, 17, LANES), f32),
            pltpu.VMEM((count, 8, LANES), f32),
            pltpu.VMEM((count, 8, LANES), f32),
            pltpu.VMEM((degrees, total_rad * LANES), f32),
            pltpu.VMEM((3, total_lat, LANES), f32),
            dma((steps, 2, CHUNKS)), dma((steps, 2, CHUNKS)),
            dma((steps, 2, r_dev)), dma((steps, 2, r_dev)),
        ] + [dma((count,))] * 6,
        compiler_params=pltpu.CompilerParams(
            collective_id=2, has_side_effects=True, vmem_limit_bytes=40 << 20
        ),
    )(*operands)
    return deliver(out)


def fits(lat_dev, r_dev, total_lat, total_rad, rad_n, count, degrees):
    width = 2 * MODES // count
    return (
        rad_n == 2
        and lat_dev == 16
        and width * count == 2 * MODES
        and width * total_rad == LANES
        and rad_n * lat_dev * r_dev == LANES
        and total_rad * (degrees * rad_n // count) == LANES
        and total_rad % 8 == 0
        and r_dev <= 8
        and degrees == 2 * LANES
        and total_lat == 2 * LANES
    )


def per_device(
    displacement, memory, ice_class, material, mu_table, decay_table, contrast_table, gravity_kernel
):
    lat_dev, r_dev, nlon = displacement.shape
    lat_count = lax.axis_size("lat")
    rad_count = lax.axis_size("rad")
    rad_index = lax.axis_index("rad")
    total_lat = lat_count * lat_dev
    total_rad = rad_count * r_dev
    degrees = gravity_kernel.shape[0] * lat_count
    cols = 2 * MODES
    columns = cols // lat_count
    stiff = lookup(material.T, mu_table)[:, :, None]
    decay = lookup(material.T, decay_table)[:, :, None]
    contrast = lookup(material.T, contrast_table)[:, :, None]
    layer_pos = (rad_index * r_dev + jnp.arange(r_dev, dtype=jnp.int32) + 1).astype(
        jnp.float32
    ) / total_rad
    source = load_scale * ice_class.astype(jnp.float32)[None, :, :] * layer_pos[:, None, None]
    devices = lat_count * rad_count
    if fits(lat_dev, r_dev, total_lat, total_rad, rad_count, devices, degrees):
        tables = (mu_table, decay_table, contrast_table)
        return fused(
            displacement, memory, ice_class, material, tables, gravity_kernel
        )
    basis, weighted = legendre(total_lat, degrees)
    projection = jnp.asarray(
        np.concatenate([weighted, np.ones((8, total_lat))]).astype(np.float32)
    )
    weight_sum = jnp.asarray(weighted.sum(axis=1).astype(np.float32))
    basis = jnp.asarray(basis.T.astype(np.float32))
    table = fourier_table(nlon, MODES)
    field, mem, kernel_every = sweeps(
        3,
        displacement.transpose(1, 0, 2),
        memory.transpose(1, 0, 2),
        source,
        stiff,
        decay,
        gravity_kernel.reshape(gravity_kernel.shape[0], -1),
    )
    kernel_every = kernel_every.reshape((degrees,) + gravity_kernel.shape[1:])
    rho = contrast * field
    spectra = jnp.dot(rho.reshape(lat_dev * r_dev, nlon), table, precision=HIGH)
    spread = lax.all_to_all(
        spectra.reshape(r_dev, lat_dev, cols).transpose(1, 0, 2), "lat", split_axis=2, concat_axis=0, tiled=True
    )
    coef_cols = jnp.dot(
        projection, spread.reshape(total_lat, r_dev * columns), precision=HIGH
    ).reshape(degrees + 8, r_dev, columns)
    coef_all = lax.all_gather(coef_cols, "rad", axis=1, tiled=True)
    first_order = (lax.axis_index("lat") * columns + jnp.arange(columns, dtype=jnp.int32)) == 0
    mean_row = jnp.sum(coef_all[degrees], axis=0) / (total_lat * total_rad)
    mean_row = jnp.where(first_order, mean_row, 0.0)
    coef_all = coef_all[:degrees] - weight_sum[:, None, None] * mean_row[None, None, :]
    phi_cols = jnp.sum(kernel_every[:, :, :, None] * coef_all[:, None, :, :], axis=2)
    synth_cols = jnp.dot(
        basis, phi_cols.reshape(degrees, r_dev * columns), precision=HIGH
    ).reshape(total_lat, r_dev, columns)
    synth = lax.all_to_all(synth_cols, "lat", split_axis=0, concat_axis=2, tiled=True)
    potential = lax.dot_general(
        synth.transpose(1, 0, 2).reshape(r_dev * lat_dev, cols), table, (((1,), (1,)), ((), ())), precision=HIGH
    ).reshape(r_dev, lat_dev, nlon)
    loaded = source + coupling * potential
    field, mem = sweeps(3, field, mem, loaded, stiff, decay)
    return tuple(x.transpose(1, 0, 2) for x in (field, mem, potential))


def solution(mesh):
    placed = (
        P("lat", "rad", None),
        P("lat", "rad", None),
        P("lat", None),
        P("lat", "rad"),
        P(),
        P(),
        P(),
        P("lat", "rad", None),
    )
    return jax.shard_map(
        per_device,
        mesh=mesh,
        in_specs=placed,
        out_specs=(P("lat", "rad", None), P("lat", "rad", None), P("lat", "rad", None)),
        check_vma=False,
    )
```

```python
import jax
import jax.numpy as jnp
import numpy as np
from jax import lax
from jax.experimental import pallas as pl
from jax.experimental.pallas import tpu as pltpu
from jax.sharding import PartitionSpec as P

MODES = 256


load_scale = 0.5
kappa_shift = 0.5
relax_factor = 0.8
coupling = 2.0
HIGH = lax.Precision.HIGH


def lookup(material, table):
    onehot = (
        material[:, :, None] == jnp.arange(table.shape[0], dtype=jnp.int32)[None, None, :]
    ).astype(jnp.float32)
    return jnp.sum(onehot * table[None, None, :], axis=-1)


def fourier_parts(nlon, modes, minor=128):
    order = np.arange(modes)
    parts = []
    for place in (np.arange(nlon // minor) * minor, np.arange(minor)):
        angle = (place[:, None] * order[None, :] % nlon) * (2.0 * np.pi / nlon)
        parts += [np.cos(angle), np.sin(angle)]
    scale = np.sqrt(2.0 / nlon)
    return [(part * f).astype(np.float32) for part, f in zip(parts, (scale, scale, 1.0, 1.0))]


def fourier_table(nlon, modes):
    ca, sa, cb, sb = lax.optimization_barrier([jnp.asarray(p) for p in fourier_parts(nlon, modes)])
    ca, sa, cb, sb = ca[:, None], sa[:, None], cb[None], sb[None]
    cos = (ca * cb - sa * sb).reshape(nlon, modes)
    sin = (sa * cb + ca * sb).reshape(nlon, modes)
    return jnp.concatenate([cos, sin], axis=1)


def legendre(lat, degrees):
    theta = np.pi * (np.arange(lat) + 0.5) / lat
    cosine = np.cos(theta)
    before, current, rows = np.zeros(lat), np.ones(lat), []
    for n in range(degrees):
        rows.append(current * np.sqrt(n + 0.5))
        before, current = current, ((2.0 * n + 1.0) * cosine * current - n * before) / (n + 1.0)
    basis = np.stack(rows)
    weighted = basis * (np.pi / lat * np.sin(theta))[None, :]
    return basis, weighted


def sweeps_kernel(steps, gather, *refs):
    if gather:
        f_ref, m_ref, s_ref, stiff_ref, decay_ref, g_ref, f_out, m_out, g_out, *refs = refs
        f_buf, face, lat_in, rad_in, send, recv, g_in, g_send, g_recv = refs
    else:
        f_ref, m_ref, s_ref, stiff_ref, decay_ref, f_out, m_out, *refs = refs
        f_buf, face, lat_in, rad_in, send, recv = refs
    layers, rows, nlon = f_ref.shape
    lat_n, rad_n = lax.axis_size("lat"), lax.axis_size("rad")
    lat, rad = lax.axis_index("lat"), lax.axis_index("rad")
    north = (lax.rem(lat + lat_n - 1, lat_n), rad)
    south = (lax.rem(lat + 1, lat_n), rad)
    below = (lat, lax.rem(rad + rad_n - 1, rad_n))
    above = (lat, lax.rem(rad + 1, rad_n))
    if gather:
        peers = [(lax.rem(lat + d, lat_n), rad) for d in range(1, lat_n)] + [below, above]
    else:
        peers = [north, south, below, above]
    barrier = pltpu.get_barrier_semaphore()
    for peer in peers:
        pl.semaphore_signal(barrier, inc=1, device_id=peer, device_id_type=pl.DeviceIdType.MESH)
    pl.semaphore_wait(barrier, len(peers))

    def remote(src, dst, send_sem, recv_sem, peer):
        copy = pltpu.make_async_remote_copy(
            src_ref=src, dst_ref=dst, send_sem=send_sem, recv_sem=recv_sem,
            device_id=peer, device_id_type=pl.DeviceIdType.MESH,
        )
        copy.start()
        return copy

    weight = relax_factor / (6.0 + kappa_shift)
    w_north = jnp.where(lat > 0, weight, 0.0)
    w_south = jnp.where(lat < lat_n - 1, weight, 0.0)
    w_below = jnp.where(rad > 0, weight, 0.0)
    w_above = jnp.where(rad < rad_n - 1, weight, 0.0)
    row = lax.broadcasted_iota(jnp.int32, (rows, nlon), 0)
    gathered = []
    for step in range(steps):
        old = f_ref if step == 0 else f_buf.at[step - 1]
        new = f_out if step == steps - 1 else f_buf.at[step]
        old_m = m_ref if step == 0 else m_out
        for r in range(layers):
            face[step, 0, r : r + 1, :] = old[r, 0:1, :]
            face[step, 1, r : r + 1, :] = old[r, rows - 1 : rows, :]
        copies = [
            remote(old.at[0], rad_in.at[step, 1], send.at[step, 0], recv.at[step, 0], below),
            remote(old.at[layers - 1], rad_in.at[step, 0], send.at[step, 1], recv.at[step, 1], above),
            remote(face.at[step, 0], lat_in.at[step, 1], send.at[step, 2], recv.at[step, 2], north),
            remote(face.at[step, 1], lat_in.at[step, 0], send.at[step, 3], recv.at[step, 3], south),
        ]
        if gather and step == 0:
            gathered = [
                remote(g_ref, g_in.at[lat], g_send.at[d], g_recv.at[d], peers[d - 1])
                for d in range(1, lat_n)
            ]
        for r in range(layers):
            f, m = old[r], old_m[r]
            beside = pltpu.roll(f, 1, 1) + pltpu.roll(f, nlon - 1, 1)
            beside += jnp.where(row == 0, 0.0, pltpu.roll(f, 1, 0))
            beside += jnp.where(row == rows - 1, 0.0, pltpu.roll(f, rows - 1, 0))
            if r > 0:
                beside += old[r - 1]
            if r < layers - 1:
                beside += old[r + 1]
            stiff = stiff_ref[r]
            update = (s_ref[r] - m) * (weight / stiff) - relax_factor * f + weight * beside
            new[r] = f + update
            m_out[r] = decay_ref[r] * m + stiff * update
        for copy in copies:
            copy.wait()
        for r, slot, w in ((0, 0, w_below), (layers - 1, 1, w_above)):
            extra = w * rad_in[step, slot]
            new[r] += extra
            m_out[r] += stiff_ref[r] * extra
        for r in range(layers):
            for j, slot, w in ((0, 0, w_north), (rows - 1, 1, w_south)):
                extra = w * lat_in[step, slot, r : r + 1, :]
                new[r, j : j + 1, :] += extra
                m_out[r, j : j + 1, :] += stiff_ref[r, j : j + 1, :] * extra
    if gather:
        for copy in gathered:
            copy.wait()
        g_in[lat] = g_ref[...]
        g_out[...] = g_in[...]


def sweeps(steps, field, memory, source, stiff, decay, gravity=None):
    gather = gravity is not None
    layers, rows, nlon = field.shape
    block = jax.ShapeDtypeStruct(field.shape, jnp.float32)
    operands, out = [field, memory, source, stiff, decay], [block, block]
    dma, f32 = pltpu.SemaphoreType.DMA, jnp.float32
    scratch = [
        pltpu.VMEM((steps - 1, layers, rows, nlon), f32),
        pltpu.VMEM((steps, 2, layers, nlon), f32),
        pltpu.VMEM((steps, 2, layers, nlon), f32),
        pltpu.VMEM((steps, 2, rows, nlon), f32),
        dma((steps, 4)),
        dma((steps, 4)),
    ]
    if gather:
        lat_n = lax.axis_size("lat")
        every = (lat_n,) + gravity.shape
        operands.append(gravity)
        out.append(jax.ShapeDtypeStruct(every, f32))
        scratch += [pltpu.VMEM(every, f32), dma((lat_n,)), dma((lat_n,))]
    vmem = pl.BlockSpec(memory_space=pltpu.VMEM)

    def kernel(*refs):
        sweeps_kernel(steps, gather, *refs)

    return pl.pallas_call(
        kernel,
        out_shape=out,
        in_specs=[vmem] * len(operands),
        out_specs=[vmem] * len(out),
        scratch_shapes=scratch,
        compiler_params=pltpu.CompilerParams(
            collective_id=0 if gather else 1, has_side_effects=True
        ),
    )(*operands)


LANES = 128
CHUNKS = 4
SWEEPS = 3


def split_np(x):
    x = np.asarray(x, np.float32)
    hi = x.astype(jnp.bfloat16)
    return hi, (x - hi.astype(np.float32)).astype(jnp.bfloat16)


def split(x):
    hi = x.astype(jnp.bfloat16)
    return hi, (x - hi.astype(jnp.float32)).astype(jnp.bfloat16)


def dot3(left, right, transposed=False):
    dims = (((1,), (1 if transposed else 0,)), ((), ()))

    def one(a, b):
        return lax.dot_general(a, b, dims, preferred_element_type=jnp.float32)

    return one(left[0], right[0]) + (one(left[0], right[1]) + one(left[1], right[0]))


def radix_tables(nlon, modes):
    quarter, per = nlon // 4, modes // 4
    place = np.arange(quarter)[:, None]

    def waves(k):
        order = k + 4 * np.arange(per)[None, :]
        angle = (place * order % nlon) * (2.0 * np.pi / nlon)
        return np.sqrt(2.0 / nlon) * np.cos(angle), np.sqrt(2.0 / nlon) * np.sin(angle)

    (c0, s0), (c1, s1), (c2, s2), (c3, s3) = (waves(k) for k in range(4))
    even = np.concatenate([c0, s0, c2, s2], axis=1)
    odd = np.concatenate(
        [np.concatenate([c1, s1, c3, s3], axis=1), np.concatenate([-s1, c1, s3, -c3], axis=1)],
        axis=0,
    )
    return even, odd


def column_orders(modes):
    per = np.arange(modes // 4)
    return np.concatenate([k + 4 * per for k in (0, 0, 2, 2, 1, 1, 3, 3)])


def swap_groups(parts, width):
    parts, step = list(parts), 1
    lane = lax.broadcasted_iota(jnp.int32, parts[0].shape, 1)
    while step < len(parts):
        low = (lane // (width * step)) % 2 == 0
        for g in range(len(parts)):
            if (g // step) % 2 == 0:
                a, b = parts[g], parts[g + step]
                parts[g] = jnp.where(low, a, pltpu.roll(b, width * step, 1))
                parts[g + step] = jnp.where(low, pltpu.roll(a, LANES - width * step, 1), b)
        step *= 2
    return parts


def fused_kernel(
    u_ref, m_ref, ice_hbm, material_hbm, gravity_hbm, mu_hbm, dec_hbm, con_hbm, shift_hbm, table_hbm,
    u_out, m_out, p_out,
    ice_ref, material, gravity, mu_ref, dec_ref, con_ref, shift_ref, pad,
    stiff_ref, decay_ref, grav_ref,
    even_hi, even_lo, odd_hi, odd_lo, fwd_hi, fwd_lo, inv_hi, inv_lo, load_sem,
    ubuf, sbuf, x_in, lat_out, lat_in, g_in, pack_out, pack_in,
    back_out, back_in, gexp, par,
    x_send, x_recv, l_send, l_recv, g_send, g_recv, a_send, a_recv, b_send, b_recv,
):
    f32 = jnp.float32
    rows, layers, nlon = u_ref.shape
    lat_n, rad_n = lax.axis_size("lat"), lax.axis_size("rad")
    lat, rad = lax.axis_index("lat"), lax.axis_index("rad")
    count = lat_n * rad_n
    me = lat * rad_n + rad
    total_lat, total_rad = lat_n * rows, rad_n * layers
    halves = rows // 8
    width = LANES // (halves * layers)
    tiles = count * width // LANES
    per_tile = LANES // width
    chunk = nlon // CHUNKS
    last = 2 * SWEEPS
    weight = relax_factor / (6.0 + kappa_shift)

    def device(index):
        return (lax.div(index, rad_n), lax.rem(index, rad_n))

    def peer(d):
        return lax.rem(me + d, count)

    barrier = pltpu.get_barrier_semaphore()

    def greet(d, carry):
        pl.semaphore_signal(
            barrier, inc=1, device_id=device(peer(d)), device_id_type=pl.DeviceIdType.MESH
        )
        return carry

    lax.fori_loop(1, count, greet, 0)

    pairs = [(u_ref.at[:, r, :], ubuf.at[0, r]) for r in range(layers)]
    pairs += [(m_ref.at[:, r, :], m_out.at[r]) for r in range(layers)]
    pairs += [
        (ice_hbm, ice_ref), (material_hbm, material), (gravity_hbm, gravity), (mu_hbm, mu_ref),
        (dec_hbm, dec_ref), (con_hbm, con_ref), (shift_hbm, shift_ref),
    ]
    first = len(pairs)
    at = 0
    for held in (even_hi, even_lo, odd_hi, odd_lo, fwd_hi, fwd_lo, inv_hi, inv_lo):
        pairs.append((table_hbm.at[pl.ds(at, held.shape[0])], held))
        at += held.shape[0]
    loads = [pltpu.make_async_copy(a, b, load_sem.at[n]) for n, (a, b) in enumerate(pairs)]
    for load in loads:
        load.start()

    def remote(src, dst, send_sem, recv_sem, target):
        return pltpu.make_async_remote_copy(
            src_ref=src, dst_ref=dst, send_sem=send_sem, recv_sem=recv_sem,
            device_id=target, device_id_type=pl.DeviceIdType.MESH,
        )

    def to_all(src_of, dst, send_sem, recv_sem):
        def start(d, carry):
            far = d // 2
            d = count // 2 + jnp.where(lax.rem(d, 2) == 1, far, -far)
            q = peer(d)
            remote(src_of(q), dst.at[me], send_sem.at[d], recv_sem.at[d], device(q)).start()
            return carry

        lax.fori_loop(1, count, start, 0)

    def each(src_of, dst, send_sem, recv_sem, how):
        other = device(peer(1))

        def wait(d, carry):
            copy = remote(src_of(me), dst.at[me], send_sem.at[d], recv_sem.at[d], other)
            copy.wait_recv() if how == "recv" else copy.wait_send()
            return carry

        lax.fori_loop(1, count, wait, 0)

    sides = (
        (0, rad > 0, 0, (lat, jnp.maximum(rad - 1, 0))),
        (1, rad < rad_n - 1, layers - 1, (lat, jnp.minimum(rad + 1, rad_n - 1))),
    )

    def x_copy(s, side, k, r, target):
        cols = pl.ds(k * chunk, chunk)
        return remote(
            ubuf.at[s, r, :, cols], x_in.at[s, 1 - side, :, cols],
            x_send.at[s, side, k], x_recv.at[s, 1 - side, k], target,
        )

    poles = (
        (0, lat > 0, 0, (jnp.maximum(lat - 1, 0), rad)),
        (1, lat < lat_n - 1, rows - 1, (jnp.minimum(lat + 1, lat_n - 1), rad)),
    )

    def lat_copy(s, side, r, target):
        return remote(
            lat_out.at[s, side, r], lat_in.at[s, 1 - side, r],
            l_send.at[s, side, r], l_recv.at[s, 1 - side, r], target,
        )

    def send_lat(s, r):
        for side, there, j, target in poles:
            @pl.when(there)
            def _():
                lat_out[s, side, r] = ubuf[s, r, j : j + 1, :]
                lat_copy(s, side, r, target).start()

    def sweep(s, more):
        row = lax.broadcasted_iota(jnp.int32, (rows, nlon), 0)

        def forward(r, when):
            if not more:
                return

            @pl.when(when)
            def _():
                send_lat(s + 1, r)

        def arrived(r):
            for side, there, _, target in poles:
                @pl.when(there)
                def _():
                    lat_copy(s, 1 - side, r, target).wait_recv()

        def inner(r, north, south):
            f, m = ubuf[s, r], m_out[r]
            beside = pltpu.roll(f, 1, 1) + pltpu.roll(f, nlon - 1, 1)
            beside += jnp.where(row == 0, north, pltpu.roll(f, 1, 0))
            beside += jnp.where(row == rows - 1, south, pltpu.roll(f, rows - 1, 0))
            if r > 0:
                beside += ubuf[s, r - 1]
            if r < layers - 1:
                beside += ubuf[s, r + 1]
            stiff = stiff_ref[r]
            update = (sbuf[r] - m) * (weight / stiff) - relax_factor * f + weight * beside
            ubuf[s + 1, r] = f + update
            m_out[r] = decay_ref[r] * m + stiff * update

        def middle(r):
            arrived(r)
            inner(r, lat_in[s, 0, r], lat_in[s, 1, r])
            forward(r, True)

        between = list(range(1, layers - 1))
        edges = [(r, there) for _, there, r, _ in sides]
        for r, _ in edges:
            inner(r, 0.0, 0.0)
        middle(between.pop(0))
        for r, there in edges:
            arrived(r)
            for side, _, j, _ in poles:
                extra = weight * lat_in[s, side, r]
                ubuf[s + 1, r, j : j + 1, :] += extra
                m_out[r, j : j + 1, :] += stiff_ref[r, j : j + 1, :] * extra
            forward(r, jnp.logical_not(there))
        for k in range(CHUNKS):
            for side, there, r, target in sides:
                @pl.when(there)
                def _():
                    cols = slice(k * chunk, (k + 1) * chunk)
                    x_copy(s, 1 - side, k, r, target).wait_recv()
                    extra = weight * x_in[s, side, :, cols]
                    ubuf[s + 1, r, :, cols] += extra
                    m_out[r, :, cols] += stiff_ref[r] * extra
                    if more:
                        x_copy(s + 1, side, k, r, target).start()
            if k < len(between):
                middle(between[k])

        for side, there, r, _ in sides:
            forward(r, there)

    for side, there, _, _ in poles:
        @pl.when(jnp.logical_not(there))
        def _():
            for s in range(last):
                lat_in[s, side] = jnp.zeros(lat_in.shape[2:], f32)
    for load in loads[:first]:
        load.wait()
    pad[...] = jnp.zeros_like(pad)
    pad[0, :layers, :rows] = material[...].astype(f32)
    own = gravity.shape[2]
    for r in range(layers):
        pad[1 + r, :, :own] = gravity[r]
    prow = lax.broadcasted_iota(jnp.int32, (rows, LANES), 0)
    plane = lax.broadcasted_iota(jnp.int32, (rows, LANES), 1)
    line = jnp.zeros((1, LANES), f32)
    for r in range(layers):
        kind = pad[0, r : r + 1]
        for x in range(rad_n):
            at = (x * layers + r) * rows
            line += jnp.where(rad == x, pltpu.roll(kind, at, 1) if at else kind, 0.0)
        column = jnp.sum(jnp.where(prow == plane, kind, 0.0), axis=1, keepdims=True)
        for table, held in ((mu_ref, stiff_ref), (dec_ref, decay_ref)):
            value = jnp.zeros((rows, 1), f32)
            for k in range(table.shape[0]):
                value = jnp.where(column == k, table[k], value)
            held[r] = value
        full = pad[1 + r]
        step = own
        while step < LANES:
            full = full + pltpu.roll(full, step, 1)
            step *= 2
        keep = lax.broadcasted_iota(jnp.int32, full.shape, 1) // own == lax.broadcasted_iota(
            jnp.int32, full.shape, 0
        )
        grav_ref[r : r + 1] = jnp.sum(jnp.where(keep, full, 0.0), axis=0, keepdims=True)
    grav_ref[layers : layers + 1] = line
    g_in[me] = grav_ref[...]
    ice = ice_ref[...].astype(f32)
    for r in range(layers):
        pos = (rad * layers + (r + 1)).astype(f32) / total_rad
        sbuf[r] = (load_scale * pos) * ice
    for load in loads[first : first + 4]:
        load.wait()

    quarter = nlon // 4
    block = layers * rows

    def piece(a):
        cols = slice(a * quarter, (a + 1) * quarter)
        return jnp.concatenate(
            [
                ubuf[0, :, :, cols].reshape(block, quarter),
                m_out[:, :, cols].reshape(block, quarter),
                ice_ref[:, cols].astype(f32),
            ],
            axis=0,
        )

    x0, x1, x2, x3 = (piece(a) for a in range(4))
    half = even_hi.shape[1] // 2
    both, diff = x0 + x2, x1 + x3
    odd = split(jnp.concatenate([x0 - x2, x1 - x3], axis=1))
    spectra = jnp.concatenate(
        [
            dot3(split(both + diff), (even_hi[:, :half], even_lo[:, :half])),
            dot3(split(both - diff), (even_hi[:, half:], even_lo[:, half:])),
            dot3(odd, (odd_hi[...], odd_lo[...])),
        ],
        axis=1,
    )

    pl.semaphore_wait(barrier, count - 1)
    for k in range(CHUNKS):
        for side, there, r, target in sides:
            @pl.when(there)
            def _():
                x_copy(0, side, k, r, target).start()
    for r in range(layers):
        send_lat(0, r)
    to_all(lambda q: grav_ref, g_in, g_send, g_recv)

    parts = []
    for h in range(halves):
        for r in range(layers):
            at = r * rows + 8 * h
            parts.append(
                jnp.concatenate(
                    [
                        spectra[o + at : o + at + 8, t * LANES : (t + 1) * LANES]
                        for t in range(tiles)
                        for o in (0, block)
                    ],
                    axis=0,
                )
            )
    for p, part in enumerate(swap_groups(parts, width)):
        for t in range(tiles):
            pack_out[per_tile * t + p, 0:16] = part[16 * t : 16 * (t + 1)]

    sub8 = lax.broadcasted_iota(jnp.int32, (8, LANES), 0)
    group8 = lax.broadcasted_iota(jnp.int32, (8, LANES), 1) // width
    for t in range(tiles):
        cols = slice(t * LANES, (t + 1) * LANES)
        x = spectra[2 * block : 2 * block + 8, cols]
        for h in range(1, halves):
            at = 2 * block + 8 * h
            x = jnp.where(rad == h, spectra[at : at + 8, cols], x)
        for step in (1, 2, 4):
            sb, gb = (sub8 // step) % 2, (group8 // step) % 2
            up = pltpu.roll(pltpu.roll(x, 8 - step, 0), width * step, 1)
            down = pltpu.roll(pltpu.roll(x, step, 0), LANES - width * step, 1)
            x = jnp.where(sb == gb, x, jnp.where(gb == 1, up, down))
        for p in range(per_tile):
            pack_out[per_tile * t + p, 16:17] = x[p : p + 1]
    to_all(lambda q: pack_out.at[q], pack_in, a_send, a_recv)
    pack_in[me] = pack_out[me]

    each(lambda q: grav_ref, g_in, g_send, g_recv, "recv")
    degrees = fwd_hi.shape[0]
    own = degrees // lat_n
    cut = lax.rem(lax.broadcasted_iota(jnp.int32, (own, LANES), 1), own) == (
        lax.broadcasted_iota(jnp.int32, (own, LANES), 0)
    )
    wide = []
    for x in range(rad_n):
        for r in range(layers):
            wide.append(
                jnp.concatenate(
                    [
                        jnp.where(
                            cut, jnp.broadcast_to(g_in[rad_n * i + x, r : r + 1], (own, LANES)), 0.0
                        )
                        for i in range(lat_n)
                    ],
                    axis=0,
                )
            )
    wide = split(jnp.concatenate(wide, axis=1))
    entries = total_rad * total_rad
    gather = jnp.where(
        lax.broadcasted_iota(jnp.int32, (wide[0].shape[1], entries), 0) // own
        == lax.broadcasted_iota(jnp.int32, (wide[0].shape[1], entries), 1),
        1.0, 0.0,
    ).astype(jnp.bfloat16)
    wide = split(
        jnp.dot(wide[0], gather, preferred_element_type=f32)
        + jnp.dot(wide[1], gather, preferred_element_type=f32)
    )
    entry = lax.broadcasted_iota(jnp.int32, (entries, LANES), 0)
    target = lax.broadcasted_iota(jnp.int32, (entries, LANES), 1) // width
    for d in range(total_rad):
        cols = slice(d * LANES, (d + 1) * LANES)
        origin = lax.rem(target + (total_rad - d), total_rad)
        place = jnp.where(entry == target * total_rad + origin, 1.0, 0.0).astype(jnp.bfloat16)
        gexp[:, cols] = jnp.dot(wide[0], place, preferred_element_type=f32) + jnp.dot(
            wide[1], place, preferred_element_type=f32
        )

    jrow = lax.broadcasted_iota(jnp.int32, (rows, LANES), 0)
    jlane = (lax.broadcasted_iota(jnp.int32, (rows, LANES), 1)) % rows
    ids = []
    for i in range(lat_n):
        line = g_in[rad_n * i, layers : layers + 1]
        for x in range(1, rad_n):
            line = line + g_in[rad_n * i + x, layers : layers + 1]
        ids.append(jnp.where(jrow == jlane, jnp.broadcast_to(line, (rows, LANES)), 0.0))
    source_layer = lax.broadcasted_iota(jnp.int32, (LANES, LANES), 0)
    source_layer = source_layer // rows
    spread = jnp.where(
        source_layer == lax.broadcasted_iota(jnp.int32, (LANES, LANES), 1) // width, 1.0, 0.0
    ).astype(jnp.bfloat16)
    ids = jnp.dot(
        jnp.concatenate(ids, axis=0).astype(jnp.bfloat16), spread,
        preferred_element_type=f32,
    )
    for n, table in enumerate((mu_ref, dec_ref, con_ref)):
        value = jnp.zeros((total_lat, LANES), f32)
        for k in range(table.shape[0]):
            value = jnp.where(ids == k, table[k], value)
        par[n] = value

    def two(s, carry):
        sweep(s, True)
        return carry

    lax.fori_loop(0, 1, two, 0)

    for load in loads[first + 4 :]:
        load.wait()
    each(lambda q: pack_out.at[q], pack_in, a_send, a_recv, "recv")
    near = lax.broadcasted_iota(jnp.int32, (16, LANES), 1) < LANES // 2
    us, qs, ss = [], [], []
    sub = lax.broadcasted_iota(jnp.int32, (8, LANES), 0)
    for i in range(lat_n):
        a, b = pack_in[rad_n * i, 0:16], pack_in[rad_n * i + 1, 0:16]
        top = jnp.where(near, a, pltpu.roll(b, LANES // 2, 1))
        low = jnp.where(near, pltpu.roll(a, LANES // 2, 1), b)
        us += [top[:8], low[:8]]
        qs += [top[8:], low[8:]]
        for x in range(rad_n):
            ss.append(
                jnp.where(
                    sub == group8,
                    jnp.broadcast_to(pack_in[rad_n * i + x, 16:17], (8, LANES)),
                    0.0,
                )
            )
    u, q, s_hat = (jnp.concatenate(v, axis=0) for v in (us, qs, ss))
    step = width
    while step < LANES:
        s_hat = s_hat + pltpu.roll(s_hat, step, 1)
        step *= 2
    glane = lax.broadcasted_iota(jnp.int32, (total_lat, LANES), 1)
    grow = lax.broadcasted_iota(jnp.int32, (total_lat, LANES), 0)
    s_hat = s_hat * ((glane // width + 1).astype(f32) * (load_scale / total_rad))
    shift = shift_ref[pl.ds(me, 1), :]
    stiff, decay, contrast = par[0], par[1], par[2]
    scaled = weight / stiff
    for n in range(SWEEPS):
        beside = shift * u
        beside += jnp.where(grow == 0, 0.0, pltpu.roll(u, 1, 0))
        beside += jnp.where(grow == total_lat - 1, 0.0, pltpu.roll(u, total_lat - 1, 0))
        beside += jnp.where(glane < width, 0.0, pltpu.roll(u, width, 1))
        beside += jnp.where(glane >= LANES - width, 0.0, pltpu.roll(u, LANES - width, 1))
        update = (s_hat - q) * scaled - relax_factor * u + weight * beside
        u = u + update
        q = decay * q + stiff * update
    rho = contrast * u
    zero = jnp.logical_and(me == 0, lax.rem(glane, width) == 0)
    mean = jnp.sum(jnp.where(zero, rho, 0.0)) / (total_lat * total_rad)
    rho = rho - jnp.where(zero, mean, 0.0)
    coef = dot3((fwd_hi[...], fwd_lo[...]), split(rho))
    phi = gexp[:, :LANES] * coef
    for d in range(1, total_rad):
        phi += gexp[:, d * LANES : (d + 1) * LANES] * pltpu.roll(coef, width * d, 1)
    synth = dot3((inv_hi[...], inv_lo[...]), split(phi))
    near8 = lax.broadcasted_iota(jnp.int32, (8, LANES), 1) < LANES // 2
    for i in range(lat_n):
        a, b = synth[rows * i : rows * i + 8], synth[rows * i + 8 : rows * i + 16]
        back_out[rad_n * i] = jnp.where(near8, a, pltpu.roll(b, LANES // 2, 1))
        back_out[rad_n * i + 1] = jnp.where(near8, pltpu.roll(a, LANES // 2, 1), b)
    to_all(lambda q: back_out.at[q], back_in, b_send, b_recv)
    back_in[me] = back_out[me]

    lax.fori_loop(1, SWEEPS, two, 0)

    each(lambda q: grav_ref, g_in, g_send, g_recv, "send")
    each(lambda q: pack_out.at[q], pack_in, a_send, a_recv, "send")
    each(lambda q: back_out.at[q], back_in, b_send, b_recv, "recv")
    parts = swap_groups(
        [
            jnp.concatenate([back_in[per_tile * t + p] for t in range(tiles)], axis=0)
            for p in range(per_tile)
        ],
        width,
    )
    lines = []
    for r in range(layers):
        for h in range(halves):
            part = parts[h * layers + r]
            lines.append(
                jnp.concatenate([part[8 * t : 8 * (t + 1)] for t in range(tiles)], axis=1)
            )
    z = jnp.concatenate(lines, axis=0)
    y0 = dot3(split(z[:, :half]), (even_hi[:, :half], even_lo[:, :half]), True)
    y2 = dot3(split(z[:, half : 2 * half]), (even_hi[:, half:], even_lo[:, half:]), True)
    y13 = dot3(split(z[:, 2 * half :]), (odd_hi[...], odd_lo[...]), True)
    alpha, beta = y13[:, :quarter], y13[:, quarter:]
    plus, minus = y0 + y2, y0 - y2
    for a, value in enumerate((plus + alpha, minus + beta, plus - alpha, minus - beta)):
        cols = slice(a * quarter, (a + 1) * quarter)
        value = value.reshape(layers, rows, quarter)
        p_out[:, :, cols] = value
        sbuf[:, :, cols] += coupling * value

    lax.fori_loop(SWEEPS, last - 1, two, 0)

    each(lambda q: back_out.at[q], back_in, b_send, b_recv, "send")

    def drain(s, carry):
        for side, there, r, target in sides:
            @pl.when(there)
            def _():
                for k in range(CHUNKS):
                    x_copy(s, side, k, r, target).wait_send()
        for side, there, _, target in poles:
            @pl.when(there)
            def _():
                for r in range(layers):
                    lat_copy(s, side, r, target).wait_send()
        return carry

    lax.fori_loop(0, last - 1, drain, 0)
    sweep(last - 1, False)
    u_out[...] = ubuf[last]
    drain(last - 1, 0)


def deliver_kernel(*refs):
    count = (len(refs) - 1) // 2
    sem = refs[-1]
    copies = []
    for n in range(count):
        for r in range(refs[n].shape[0]):
            copies.append(
                pltpu.make_async_copy(refs[n].at[r], refs[count + n].at[:, r, :], sem.at[n, r])
            )
    for copy in copies:
        copy.start()
    for copy in copies:
        copy.wait()


def deliver(blocks):
    layers, rows, nlon = blocks[0].shape
    return tuple(
        pl.pallas_call(
            deliver_kernel,
            out_shape=[jax.ShapeDtypeStruct((rows, layers, nlon), jnp.float32)] * len(blocks),
            in_specs=[pl.BlockSpec(memory_space=pltpu.VMEM)] * len(blocks),
            out_specs=[pl.BlockSpec(memory_space=pltpu.HBM)] * len(blocks),
            scratch_shapes=[pltpu.SemaphoreType.DMA((len(blocks), layers))],
            compiler_params=pltpu.CompilerParams(vmem_limit_bytes=4 << 20),
        )(*blocks)
    )


def fused(displacement, memory, ice_class, material, tables, gravity):
    lat_dev, r_dev, nlon = displacement.shape
    lat_n, rad_n = lax.axis_size("lat"), lax.axis_size("rad")
    count, total_lat, total_rad = lat_n * rad_n, lat_n * lat_dev, rad_n * r_dev
    degrees = gravity.shape[0] * lat_n
    width = 2 * MODES // count
    bf16, f32 = jnp.bfloat16, jnp.float32
    even, odd = (split_np(t) for t in radix_tables(nlon, MODES))
    basis, weighted = legendre(total_lat, degrees)
    fwd, inv = split_np(weighted), split_np(basis.T)
    orders = column_orders(MODES).reshape(count, width)
    shift = np.tile(2.0 * np.cos(2.0 * np.pi * orders / nlon), (1, total_rad)).astype(np.float32)
    tabs = [*even, *odd, *fwd, *inv]
    gravity = gravity.transpose(1, 2, 0)
    operands = [
        displacement, memory, ice_class, material.T, gravity, *tables, shift, np.concatenate(tabs, axis=0)
    ]
    operands = [pltpu.with_memory_space_constraint(jnp.asarray(x), pltpu.HBM) for x in operands]
    vmem = pl.BlockSpec(memory_space=pltpu.VMEM)
    hbm = pl.BlockSpec(memory_space=pltpu.HBM)
    dma = pltpu.SemaphoreType.DMA
    steps = 2 * SWEEPS
    block = jax.ShapeDtypeStruct((r_dev, lat_dev, nlon), f32)
    out = pl.pallas_call(
        fused_kernel,
        out_shape=[block] * 3,
        in_specs=[hbm] * len(operands),
        out_specs=[vmem] * 3,
        scratch_shapes=[pltpu.VMEM(x.shape, x.dtype) for x in operands[2:5]]
        + [pltpu.SMEM(x.shape, x.dtype) for x in tables]
        + [
            pltpu.VMEM(shift.shape, f32),
            pltpu.VMEM((1 + r_dev, 8, LANES), f32),
            pltpu.VMEM((r_dev, lat_dev, 1), f32),
            pltpu.VMEM((r_dev, lat_dev, 1), f32),
            pltpu.VMEM((r_dev + 1, LANES), f32),
        ]
        + [pltpu.VMEM(x.shape, x.dtype) for x in tabs]
        + [
            dma((2 * r_dev + 7 + len(tabs),)),
            pltpu.VMEM((steps + 1, r_dev, lat_dev, nlon), f32),
            pltpu.VMEM((r_dev, lat_dev, nlon), f32),
            pltpu.VMEM((steps, 2, lat_dev, nlon), f32),
            pltpu.VMEM((steps, 2, r_dev, 1, nlon), f32),
            pltpu.VMEM((steps, 2, r_dev, 1, nlon), f32),
            pltpu.VMEM((count, r_dev + 1, LANES), f32),
            pltpu.VMEM((count, 17, LANES), f32),
            pltpu.VMEM((count, 17, LANES), f32),
            pltpu.VMEM((count, 8, LANES), f32),
            pltpu.VMEM((count, 8, LANES), f32),
            pltpu.VMEM((degrees, total_rad * LANES), f32),
            pltpu.VMEM((3, total_lat, LANES), f32),
            dma((steps, 2, CHUNKS)), dma((steps, 2, CHUNKS)),
            dma((steps, 2, r_dev)), dma((steps, 2, r_dev)),
        ] + [dma((count,))] * 6,
        compiler_params=pltpu.CompilerParams(
            collective_id=2, has_side_effects=True, vmem_limit_bytes=40 << 20
        ),
    )(*operands)
    return deliver(out)


def fits(lat_dev, r_dev, total_lat, total_rad, rad_n, count, degrees):
    width = 2 * MODES // count
    return (
        rad_n == 2
        and lat_dev == 16
        and width * count == 2 * MODES
        and width * total_rad == LANES
        and rad_n * lat_dev * r_dev == LANES
        and total_rad * (degrees * rad_n // count) == LANES
        and total_rad % 8 == 0
        and r_dev <= 8
        and degrees == 2 * LANES
        and total_lat == 2 * LANES
    )


def per_device(
    displacement, memory, ice_class, material, mu_table, decay_table, contrast_table, gravity_kernel
):
    lat_dev, r_dev, nlon = displacement.shape
    lat_count = lax.axis_size("lat")
    rad_count = lax.axis_size("rad")
    rad_index = lax.axis_index("rad")
    total_lat = lat_count * lat_dev
    total_rad = rad_count * r_dev
    degrees = gravity_kernel.shape[0] * lat_count
    cols = 2 * MODES
    columns = cols // lat_count
    stiff = lookup(material.T, mu_table)[:, :, None]
    decay = lookup(material.T, decay_table)[:, :, None]
    contrast = lookup(material.T, contrast_table)[:, :, None]
    layer_pos = (rad_index * r_dev + jnp.arange(r_dev, dtype=jnp.int32) + 1).astype(
        jnp.float32
    ) / total_rad
    source = load_scale * ice_class.astype(jnp.float32)[None, :, :] * layer_pos[:, None, None]
    devices = lat_count * rad_count
    if fits(lat_dev, r_dev, total_lat, total_rad, rad_count, devices, degrees):
        tables = (mu_table, decay_table, contrast_table)
        return fused(
            displacement, memory, ice_class, material, tables, gravity_kernel
        )
    basis, weighted = legendre(total_lat, degrees)
    projection = jnp.asarray(
        np.concatenate([weighted, np.ones((8, total_lat))]).astype(np.float32)
    )
    weight_sum = jnp.asarray(weighted.sum(axis=1).astype(np.float32))
    basis = jnp.asarray(basis.T.astype(np.float32))
    table = fourier_table(nlon, MODES)
    field, mem, kernel_every = sweeps(
        3,
        displacement.transpose(1, 0, 2),
        memory.transpose(1, 0, 2),
        source,
        stiff,
        decay,
        gravity_kernel.reshape(gravity_kernel.shape[0], -1),
    )
    kernel_every = kernel_every.reshape((degrees,) + gravity_kernel.shape[1:])
    rho = contrast * field
    spectra = jnp.dot(rho.reshape(lat_dev * r_dev, nlon), table, precision=HIGH)
    spread = lax.all_to_all(
        spectra.reshape(r_dev, lat_dev, cols).transpose(1, 0, 2), "lat", split_axis=2, concat_axis=0, tiled=True
    )
    coef_cols = jnp.dot(
        projection, spread.reshape(total_lat, r_dev * columns), precision=HIGH
    ).reshape(degrees + 8, r_dev, columns)
    coef_all = lax.all_gather(coef_cols, "rad", axis=1, tiled=True)
    first_order = (lax.axis_index("lat") * columns + jnp.arange(columns, dtype=jnp.int32)) == 0
    mean_row = jnp.sum(coef_all[degrees], axis=0) / (total_lat * total_rad)
    mean_row = jnp.where(first_order, mean_row, 0.0)
    coef_all = coef_all[:degrees] - weight_sum[:, None, None] * mean_row[None, None, :]
    phi_cols = jnp.sum(kernel_every[:, :, :, None] * coef_all[:, None, :, :], axis=2)
    synth_cols = jnp.dot(
        basis, phi_cols.reshape(degrees, r_dev * columns), precision=HIGH
    ).reshape(total_lat, r_dev, columns)
    synth = lax.all_to_all(synth_cols, "lat", split_axis=0, concat_axis=2, tiled=True)
    potential = lax.dot_general(
        synth.transpose(1, 0, 2).reshape(r_dev * lat_dev, cols), table, (((1,), (1,)), ((), ())), precision=HIGH
    ).reshape(r_dev, lat_dev, nlon)
    loaded = source + coupling * potential
    field, mem = sweeps(3, field, mem, loaded, stiff, decay)
    return tuple(x.transpose(1, 0, 2) for x in (field, mem, potential))


def solution(mesh):
    placed = (
        P("lat", "rad", None),
        P("lat", "rad", None),
        P("lat", None),
        P("lat", "rad"),
        P(),
        P(),
        P(),
        P("lat", "rad", None),
    )
    return jax.shard_map(
        per_device,
        mesh=mesh,
        in_specs=placed,
        out_specs=(P("lat", "rad", None), P("lat", "rad", None), P("lat", "rad", None)),
        check_vma=False,
    )
```
